512 devices in a mesh: gx: 4 (over x), gy: 8 (over z_hi, core), gz: 16 (over y, z_lo).
Axes of the slice: x: 4, y: 4, z: 16 (z_hi: 4, z_lo: 4; z = z_hi * 4 + z_lo), core: 2. Of those that a mesh axis runs over, the one named last changes fastest.
Arguments:
- positions: float32 [3, 8, 64, 32, 128], P(None, 'gx', 'gy', 'gz'), may hold values from 0 to 11
- velocities: float32 [3, 8, 64, 32, 128], P(None, 'gx', 'gy', 'gz'), may hold values from -6 to 6
- counts: int32 [8, 64, 32], P('gx', 'gy', 'gz'), may hold values from 64 to 128
- grid_cells: int32 [8, 64, 32, 128], P('gx', 'gy', 'gz'), may hold values from 0 to 7
- electron_temp: float32 [16, 128, 64], P('gx', ('gy', 'gz')), may hold values from 0.5 to 8
Outputs:
- velocity_out: float32 [3, 8, 64, 32, 128], P(None, 'gx', 'gy', 'gz')
- electron_out: float32 [16, 128, 64], P('gx', ('gy', 'gz'))
The draws below stay inside these ranges and needn't reach their ends.
Inputs may be any that keep to these rules, and one draw needn't show every extreme that they name: `counts`: slot k of a cell holds an atom exactly when k is below the cell's count; other slots' positions, velocities and grid cells are ignored. `grid_cells`: grid cells are numbered within the atom cell's block of 2 x 2 x 2 with z fastest.
All inputs are finite; a program needn't handle non-finite values.
Results may differ from the reference program's by a relative error of at most 0.0003.
Values sent between devices are 32-bit elements; how exact they have to be, the bound alone decides.
No kernel may reach another device: no remote copies, remote signals or barrier semaphores. Data moves between devices by JAX's collectives and lax.ppermute only.
A program may use at most 64 MiB of HBM per device.

```python
import math
import jax
import jax.numpy as jnp
from jax import lax

CAP = 128
SUBX = 2
SUBY = 2
SUBZ = 2
SUBSTEPS = 4
NCX = 8
NCY = 64
NCZ = 32
NGX = 16
NGY = 128
NGZ = 64
SUBCELLS = 8


def set_ends(array, stream_key, least, largest):
    spot = [jax.random.randint(jax.random.fold_in(stream_key, axis), (), 0, length) for axis, length in enumerate(array.shape)]
    longest = array.shape.index(max(array.shape))
    neighbour = spot[:longest] + [(spot[longest] + 1) % array.shape[longest]] + spot[longest + 1:]
    return array.at[tuple(spot)].set(least).at[tuple(neighbour)].set(largest)


def block_levels(rng, dims, pieces, least, top_value):
    loudness, own = 1.0, jax.random.fold_in(rng, 6)
    for axis_at, parts in pieces:
        heights = jnp.exp(jax.random.uniform(jax.random.fold_in(own, axis_at), (parts,), jnp.float32, least / len(pieces), top_value / len(pieces)))
        loudness = loudness * jnp.repeat(heights, dims[axis_at] // parts).reshape([-1 if axis == axis_at else 1 for axis in range(len(dims))])
    return loudness


def noise(own_key, dims, spread, bound, cuts=(), kind=jnp.bfloat16):
    array = jax.random.normal(own_key, dims, jnp.float32) * spread
    if len(cuts) > 0:
        array = block_levels(own_key, dims, cuts, -0.22, 0.18) * array
    return jnp.clip(array, min=-bound, max=bound).astype(kind)


def setup_inputs(seed: int = 0) -> dict:
    key_of = jax.random.split(jax.random.key(seed), 6)
    positions = jnp.clip(11.0 * jax.random.uniform(key_of[0], (3, NCX, NCY, NCZ, CAP), jnp.float32) ** block_levels(key_of[0], (3, NCX, NCY, NCZ, CAP), ((1, 4), (2, 8), (3, 16)), -0.2, 0.2), 0.0, 11.0)
    velocities = noise(key_of[1], (3, NCX, NCY, NCZ, CAP), 1.0, 6.0, ((1, 4), (2, 8), (3, 16)), jnp.float32)
    counts = set_ends(jax.random.randint(key_of[2], (NCX, NCY, NCZ), CAP // 2, CAP + 1), jax.random.fold_in(key_of[2], 1), CAP // 2, CAP).astype(jnp.int32)
    grid_cells = set_ends(jax.random.randint(key_of[3], (NCX, NCY, NCZ, CAP), 0, SUBCELLS), jax.random.fold_in(key_of[3], 1), 0, SUBCELLS - 1).astype(jnp.int32)
    electron_temp = jnp.clip(jnp.exp(math.log(8.0) - 2.7725887 * jax.random.uniform(key_of[4], (NGX, NGY, NGZ), jnp.float32) ** block_levels(key_of[4], (NGX, NGY, NGZ), ((0, 4), (1, 128)), -0.2, 0.2)), 0.5, 8.0)
    return {"positions": positions, "velocities": velocities, "counts": counts, "grid_cells": grid_cells, "electron_temp": electron_temp}


CELL_EDGE = 11.0
CUT_SQUARED = 30.25
EMBED_SCALE = 1.0
PAIR_SCALE = 0.5
TIME_STEP = 0.2
ATOM_MASS = 1.0
COUPLING = 0.02
LATTICE_SCALE = 1.0
SPREAD = 0.15
PHONON_RATE = 0.05
FAR_AWAY = 1000.0
FAR_STEP = 100.0
NEIGHBOUR_SHIFTS = [(shift_x, shift_y, shift_z) for shift_x in (-1, 0, 1) for shift_y in (-1, 0, 1) for shift_z in (-1, 0, 1)]

def park_atoms(positions, counts):
    capacity = positions.shape[-1]
    slot_index = lax.broadcasted_iota(jnp.int32, counts.shape + (capacity,), counts.ndim)
    occupied = slot_index < counts[..., None]
    parked = FAR_AWAY + FAR_STEP * slot_index.astype(jnp.float32)
    return (jnp.where(occupied[None], positions, parked[None]), occupied)

def separation(centre_atoms, neighbours, shift):
    deltas = [neighbours[axis_no][:, None, :] - centre_atoms[axis_no][:, :, None] + shift[axis_no] * CELL_EDGE for axis_no in range(3)]
    squared = deltas[0] * deltas[0] + deltas[1] * deltas[1] + deltas[2] * deltas[2]
    reach = jnp.maximum(1.0 - squared / CUT_SQUARED, 0.0)
    return (deltas, reach)

def densities(source):
    width_x = source.shape[1] - 2
    width_y = source.shape[2] - 2
    height = source.shape[3] - 2
    capacity = source.shape[4]
    diagonal_mask = jnp.eye(capacity, dtype=bool)
    zero = jnp.zeros((), jnp.int32)

    def column(carry, index):
        index_x = index // width_y
        index_y = index % width_y
        window = lax.dynamic_slice(source, (zero, index_x, index_y, zero, zero), (3, 3, 3, height + 2, capacity))
        centre_atoms = window[:, 1, 1, 1:height + 1]
        summed = jnp.zeros((height, capacity), jnp.float32)
        for shift in NEIGHBOUR_SHIFTS:
            neighbours = window[:, shift[0] + 1, shift[1] + 1, shift[2] + 1:shift[2] + 1 + height]
            deltas, reach = separation(centre_atoms, neighbours, shift)
            weight = reach * reach * reach
            if shift == (0, 0, 0):
                weight = jnp.where(diagonal_mask, 0.0, weight)
            summed = summed + lax.optimization_barrier(jnp.sum(weight, axis=-1))
        return (carry, summed)
    carry, stacked = lax.scan(column, zero, jnp.arange(width_x * width_y, dtype=jnp.int32))
    return stacked.reshape(width_x, width_y, height, capacity)

def forces(source, slopes):
    width_x = source.shape[1] - 2
    width_y = source.shape[2] - 2
    height = source.shape[3] - 2
    capacity = source.shape[4]
    diagonal_mask = jnp.eye(capacity, dtype=bool)
    zero = jnp.zeros((), jnp.int32)

    def column(carry, index):
        index_x = index // width_y
        index_y = index % width_y
        window = lax.dynamic_slice(source, (zero, index_x, index_y, zero, zero), (3, 3, 3, height + 2, capacity))
        slope_window = lax.dynamic_slice(slopes, (index_x, index_y, zero, zero), (3, 3, height + 2, capacity))
        centre_atoms = window[:, 1, 1, 1:height + 1]
        centre_slope = slope_window[1, 1, 1:height + 1]
        sums = [jnp.zeros((height, capacity), jnp.float32) for axis_no in range(3)]
        for shift in NEIGHBOUR_SHIFTS:
            neighbours = window[:, shift[0] + 1, shift[1] + 1, shift[2] + 1:shift[2] + 1 + height]
            neighbour_slope = slope_window[shift[0] + 1, shift[1] + 1, shift[2] + 1:shift[2] + 1 + height]
            deltas, reach = separation(centre_atoms, neighbours, shift)
            coefficient = 2.0 * reach * reach * ((centre_slope[:, :, None] + neighbour_slope[:, None, :]) * (-3.0 / CUT_SQUARED) - 3.0 * PAIR_SCALE / CUT_SQUARED)
            if shift == (0, 0, 0):
                coefficient = jnp.where(diagonal_mask, 0.0, coefficient)
            sums = [sums[axis_no] + lax.optimization_barrier(jnp.sum(coefficient * deltas[axis_no], axis=-1)) for axis_no in range(3)]
        return (carry, jnp.stack(sums))
    carry, stacked = lax.scan(column, zero, jnp.arange(width_x * width_y, dtype=jnp.int32))
    return jnp.moveaxis(stacked.reshape(width_x, width_y, 3, height, capacity), 2, 0)

def embed_slope(density):
    return -0.5 * EMBED_SCALE / jnp.sqrt(density + 1.0)

def grid_index(grid_cells, span_y, span_z):
    cell_x = lax.broadcasted_iota(jnp.int32, grid_cells.shape, 0)
    cell_y = lax.broadcasted_iota(jnp.int32, grid_cells.shape, 1)
    cell_z = lax.broadcasted_iota(jnp.int32, grid_cells.shape, 2)
    fine_x = cell_x * SUBX + grid_cells // (SUBY * SUBZ)
    fine_y = cell_y * SUBY + grid_cells // SUBZ % SUBY
    fine_z = cell_z * SUBZ + grid_cells % SUBZ
    return ((fine_x * span_y + fine_y) * span_z + fine_z).astype(jnp.int32)

def diffuse(extended, lattice):
    centre = extended[1:-1, 1:-1]
    beside = extended[2:, 1:-1] + extended[:-2, 1:-1] + extended[1:-1, 2:] + extended[1:-1, :-2]
    beside = beside + jnp.roll(centre, 1, 2) + jnp.roll(centre, -1, 2)
    return centre + SPREAD * (beside - 6.0 * centre) - PHONON_RATE * (centre - lattice)

def reference(positions, velocities, counts, grid_cells, electron_temp):
    parked, occupied = park_atoms(positions, counts)
    source = jnp.pad(parked, ((0, 0), (1, 1), (1, 1), (1, 1), (0, 0)), mode='wrap')
    density = densities(source)
    slopes = jnp.pad(embed_slope(density), ((1, 1), (1, 1), (1, 1), (0, 0)), mode='wrap')
    force_field = forces(source, slopes)
    kinetic = jnp.where(occupied, 0.5 * ATOM_MASS * lax.optimization_barrier(jnp.sum(velocities * velocities, axis=0)), 0.0)
    flat_index = grid_index(grid_cells, NGY, NGZ)
    energy = jax.ops.segment_sum(kinetic.reshape(-1), flat_index.reshape(-1), num_segments=NGX * NGY * NGZ)
    lattice = LATTICE_SCALE * energy.reshape(NGX, NGY, NGZ)
    heat_field = electron_temp
    for substep in range(SUBSTEPS):
        extended = jnp.pad(heat_field, ((1, 1), (1, 1), (0, 0)), mode='wrap')
        heat_field = diffuse(extended, lattice)
    electron_here = jnp.take(heat_field.reshape(-1), flat_index)
    lattice_here = jnp.take(lattice.reshape(-1), flat_index)
    moved = velocities + TIME_STEP / ATOM_MASS * force_field + COUPLING * (electron_here - lattice_here)[None] * velocities
    velocity_out = jnp.where(occupied[None], moved, 0.0)
    return (velocity_out, heat_field)
```

```python
import functools
import numpy as np
import jax
import jax.numpy as jnp
from jax import lax
from jax.experimental import pallas as pl
from jax.experimental.pallas import tpu as pltpu
from jax.sharding import PartitionSpec as P

CUT = 30.25
EDGE = 11.0
HALF = 5.5
BIG = 10000.0
F32 = jnp.float32
BF = jnp.bfloat16


def split3(v):
    hi = v.astype(BF).astype(F32)
    rest = v - hi
    mid = rest.astype(BF).astype(F32)
    return hi, mid, rest - mid


def shift_tables():
    m = np.zeros((27, 8, 128), np.float32)
    k = np.zeros((27, 8, 128), np.float32)
    n = 0
    for ox in (-1, 0, 1):
        for oy in (-1, 0, 1):
            for oz in (-1, 0, 1):
                o = (ox, oy, oz)
                m[n, 0:5] = 1.0
                for a in range(3):
                    m[n, 5 + a] = o[a]
                    k[n, a] = -2.0 * EDGE * o[a]
                k[n, 4] = -EDGE * EDGE * sum(abs(a) for a in o)
                n += 1
    return m, k


def cell_rows(pos_ref, x, y, z):
    px = pos_ref[0, x, y, pl.ds(z, 1), :]
    py = pos_ref[1, x, y, pl.ds(z, 1), :]
    pz = pos_ref[2, x, y, pl.ds(z, 1), :]
    empty = px > 500.0
    qx = jnp.where(empty, 0.0, px - HALF)
    qy = jnp.where(empty, 0.0, py - HALF)
    qz = jnp.where(empty, 0.0, pz - HALF)
    s = jnp.where(empty, BIG, qx * qx + qy * qy + qz * qz)
    b = lambda v: jnp.broadcast_to(v, (8, 128))
    return b(qx), b(qy), b(qz), b(s)


def pick(row, *vals):
    out = vals[-1]
    for n in range(len(vals) - 2, -1, -1):
        out = jnp.where(row == n, vals[n], out)
    return out


def neighbour_block(row, rows):
    qx, qy, qz, s = rows
    v = pick(row, qx, qy, qz, s, jnp.float32(1.0), jnp.float32(2.0 * EDGE))
    hi, mid, lo = split3(v)
    z = jnp.zeros_like(hi)
    return jnp.concatenate([hi, mid, lo, hi, mid, hi, z, z], axis=0)


def centre_block(row, rows):
    qx, qy, qz, s = rows
    return pick(row, 2.0 * qx, 2.0 * qy, 2.0 * qz, jnp.float32(-1.0), CUT - s, qx, qy, qz)


def centre_weights(d, m, k):
    u1, u2, u3 = split3(d * m + k)
    z = jnp.zeros_like(u1)
    return jnp.concatenate([u1, u1, u1, u2, u2, u3, z, z], axis=0).astype(BF)


def dot(a, b):
    return jnp.dot(a, b, preferred_element_type=F32)


def pair_values(te_ref, base, odd, c0, c1):
    z64 = jnp.zeros((64, 128), BF)
    if not odd:
        lhs = te_ref[base]
        rhs = jnp.concatenate([jnp.concatenate([c0, z64], 1), jnp.concatenate([z64, c1], 1)], 0)
    else:
        lhs = jnp.concatenate([te_ref[base], te_ref[base + 1]], 1)
        rhs = jnp.concatenate(
            [jnp.concatenate([z64, c0, z64, z64], 0), jnp.concatenate([z64, z64, c1, z64], 0)], 1)
    return jnp.maximum(dot(lhs, rhs), 0.0)


def main_kernel(EX, EY, EZ, pos_ref, vel_ref, grid_ref, diff_ref, m_ref, k_ref, out_ref, te_ref, sl_ref, g_ref):
    NP = EZ // 2
    row = lax.broadcasted_iota(jnp.int32, (8, 128), 0)
    jj = lax.broadcasted_iota(jnp.int32, (128, 256), 0)
    ii = lax.broadcasted_iota(jnp.int32, (128, 256), 1)
    diag = (jj == ii) | (jj + 128 == ii)

    def prep(n, _):
        x = n // EY
        y = n % EY
        for p in range(NP):
            a = neighbour_block(row, cell_rows(pos_ref, x, y, 2 * p))
            b = neighbour_block(row, cell_rows(pos_ref, x, y, 2 * p + 1))
            te_ref[n * NP + p] = jnp.concatenate([a, b], 0).T.astype(BF)
        return 0
    lax.fori_loop(0, EX * EY, prep, 0)

    DY = EY - 2
    DP = (EZ - 2) // 2

    def dens(n, _):
        zp = n % DP
        c = n // DP
        y = c % DY + 1
        x = c // DY + 1
        z0 = 1 + 2 * zp
        d0 = centre_block(row, cell_rows(pos_ref, x, y, z0))
        d1 = centre_block(row, cell_rows(pos_ref, x, y, z0 + 1))
        acc = jnp.zeros((8, 256), F32)
        for ox in (-1, 0, 1):
            for oy in (-1, 0, 1):
                col = ((x + ox) * EY + y + oy) * NP + zp
                for oz in (-1, 0, 1):
                    o = (ox + 1) * 9 + (oy + 1) * 3 + oz + 1
                    m, k = m_ref[o], k_ref[o]
                    c0, c1 = centre_weights(d0, m, k), centre_weights(d1, m, k)
                    r = pair_values(te_ref, col + (1 if oz == 1 else 0), oz == 0, c0, c1)
                    if o == 13:
                        r = jnp.where(diag, 0.0, r)
                    w = r * r * r
                    acc = acc + w.reshape(16, 8, 256).sum(0)
        d = jnp.sum(acc, axis=0, keepdims=True) * (1.0 / CUT ** 3)
        sl = -0.5 / jnp.sqrt(d + 1.0)
        sl_ref[x, y, pl.ds(z0, 1), :] = sl[:, :128]
        sl_ref[x, y, pl.ds(z0 + 1, 1), :] = sl[:, 128:]
        return 0
    lax.fori_loop(0, (EX - 2) * DY * DP, dens, 0)

    def gprep(n, _):
        x = n // DY + 1
        y = n % DY + 1
        for z in range(1, EZ - 1):
            qx, qy, qz, _s = cell_rows(pos_ref, x, y, z)
            s = jnp.broadcast_to(sl_ref[x, y, pl.ds(z, 1), :], (8, 128))
            r4 = row % 4
            v = pick(r4, qx, qy, qz, jnp.ones_like(qx))
            v = v * jnp.where(row < 4, 1.0, s)
            hi, mid, lo = split3(v)
            g_ref[(x * EY + y) * EZ + z] = jnp.concatenate([hi, mid, lo, jnp.zeros_like(hi)], 0).astype(BF)
        return 0
    lax.fori_loop(0, (EX - 2) * DY, gprep, 0)

    FY = EY - 4

    def force(n, _):
        y = n % FY + 2
        x = n // FY + 2
        z0 = 2
        rows0 = cell_rows(pos_ref, x, y, z0)
        rows1 = cell_rows(pos_ref, x, y, z0 + 1)
        d0, d1 = centre_block(row, rows0), centre_block(row, rows1)
        zero = jnp.zeros((8, 128), F32)
        acc = [[zero] * 4, [zero] * 4]
        for ox in (-1, 0, 1):
            for oy in (-1, 0, 1):
                colxy = (x + ox) * EY + y + oy
                for oz in (-1, 0, 1):
                    o = (ox + 1) * 9 + (oy + 1) * 3 + oz + 1
                    m, k = m_ref[o], k_ref[o]
                    c0, c1 = centre_weights(d0, m, k), centre_weights(d1, m, k)
                    L = z0 + oz
                    r = pair_values(te_ref, colxy * NP + L // 2, L % 2 == 1, c0, c1)
                    if o == 13:
                        r = jnp.where(diag, 0.0, r)
                    t = r * r
                    hi = t.astype(BF)
                    lo = (t - hi.astype(F32)).astype(BF)
                    for half in range(2):
                        ls = slice(128 * half, 128 * half + 128)
                        tt = jnp.concatenate([hi[:, ls], lo[:, ls]], 0)
                        g = g_ref[colxy * EZ + L + half]
                        f = dot(jnp.concatenate([g, g], 1), tt)
                        f8 = f[0:8] + f[8:16] + f[16:24]
                        a = acc[half]
                        a[0] = a[0] + f8
                        for ax, s in ((1, ox), (2, oy), (3, oz)):
                            if s == 1:
                                a[ax] = a[ax] + f8
                            elif s == -1:
                                a[ax] = a[ax] - f8
        for half, rows in ((0, rows0), (1, rows1)):
            a = acc[half]
            z = z0 + half
            s = sl_ref[x, y, pl.ds(z, 1), :]
            gi = grid_ref[x - 2, y - 2, pl.ds(half, 1), :]
            dl = diff_ref[(x - 2) * FY + y - 2, pl.ds(half, 1), :]
            h = jnp.zeros((1, 128), F32)
            for kk in range(8):
                h = jnp.where(gi == kk, dl[:, kk:kk + 1], h)
            occ = gi < 8
            for ax in range(3):
                q = rows[ax][0:1]
                M = a[0][ax:ax + 1] + EDGE * a[1 + ax][3:4] - q * a[0][3:4]
                N = a[0][4 + ax:5 + ax] + EDGE * a[1 + ax][7:8] - q * a[0][7:8]
                fo = (2.0 / CUT ** 2) * ((-3.0 / CUT) * (s * M + N) + (-1.5 / CUT) * M)
                v = vel_ref[ax, x - 2, y - 2, pl.ds(half, 1), :]
                o_ = v + 0.2 * fo + 0.02 * h * v
                out_ref[ax, x - 2, y - 2, pl.ds(half, 1), :] = jnp.where(occ, o_, 0.0)
        return 0
    lax.fori_loop(0, (EX - 4) * FY, force, 0)


def main_call(pos, vel, gidx, diff):
    EX, EY, EZ = pos.shape[1:4]
    m, k = shift_tables()
    vm = pl.BlockSpec(memory_space=pltpu.VMEM)
    return pl.pallas_call(
        functools.partial(main_kernel, EX, EY, EZ),
        out_shape=jax.ShapeDtypeStruct(vel.shape, F32),
        in_specs=[vm] * 6,
        out_specs=vm,
        scratch_shapes=[
            pltpu.VMEM((EX * EY * EZ // 2, 128, 128), BF),
            pltpu.VMEM((EX, EY, EZ, 128), F32),
            pltpu.VMEM((EX * EY * EZ, 32, 128), BF),
        ],
        compiler_params=pltpu.CompilerParams(vmem_limit_bytes=56 * 2 ** 20),
        name="pair_forces",
    )(pos, vel, gidx, diff, jnp.asarray(m), jnp.asarray(k))


def diffuse_kernel(EX, EY, EZ, g_ref, e_out, diff_out, e_ref):
    rows = EX * EY * EZ
    pad = EY * EZ + 8 - (EY * EZ) % 8
    lat = g_ref[...]
    e_ref[...] = jnp.zeros(e_ref.shape, F32)
    e = pltpu.roll(lat, 120, 1)
    lane = lax.broadcasted_iota(jnp.int32, (rows, 128), 1)
    for step in range(4):
        e_ref[pl.ds(pad, rows), :] = e
        beside = None
        for bit, stride in ((1, 1), (2, EZ), (4, EY * EZ)):
            after = e_ref[pl.ds(pad + stride, rows), :]
            before = e_ref[pl.ds(pad - stride, rows), :]
            low = pltpu.roll(e + before, 128 - bit, 1)
            high = pltpu.roll(e + after, bit, 1)
            s = jnp.where((lane & bit) == 0, low, high)
            beside = s if beside is None else beside + s
        e = e + 0.15 * (beside - 6.0 * e) - 0.05 * (e - lat)
    d = e - lat
    e_ref[pl.ds(pad, rows), :] = e
    for x in range(2, EX - 2):
        for y in range(2, EY - 2):
            r = (x * EY + y) * EZ + 2
            n = (x - 2) * (EY - 4) + y - 2
            e_out[n] = e[r:r + EZ - 4]
            diff_out[n] = d[r:r + EZ - 4]


def diffuse_call(grid):
    EX, EY, EZ = grid.shape[:3]
    rows = EX * EY * EZ
    pad = EY * EZ + 8 - (EY * EZ) % 8
    vm = pl.BlockSpec(memory_space=pltpu.VMEM)
    shape = jax.ShapeDtypeStruct(((EX - 4) * (EY - 4), EZ - 4, 128), F32)
    return pl.pallas_call(
        functools.partial(diffuse_kernel, EX, EY, EZ),
        out_shape=(shape, shape),
        in_specs=[vm],
        out_specs=(vm, vm),
        scratch_shapes=[pltpu.VMEM((rows + 2 * pad, 128), F32)],
        name="diffusion",
    )(grid.reshape(rows, 128))


def extend(value, sides, width):
    for axis, dim in sides:
        devices, length = lax.axis_size(axis), value.shape[dim]
        up = [(i, (i + 1) % devices) for i in range(devices)]
        down = [(j, i) for i, j in up]
        before = lax.ppermute(lax.slice_in_dim(value, length - width, length, axis=dim), axis, up)
        after = lax.ppermute(lax.slice_in_dim(value, 0, width, axis=dim), axis, down)
        value = jnp.concatenate([before, value, after], axis=dim)
    return value


def per_device(positions, velocities, counts, grid_cells, electron_temp):
    nx, ny, nz = counts.shape
    slot = lax.broadcasted_iota(jnp.int32, grid_cells.shape, 3)
    occupied = slot < counts[..., None]
    e = lax.all_to_all(electron_temp, "gz", split_axis=2, concat_axis=1, tiled=True)
    e = e.reshape(nx, 2, ny, 2, nz, 2).transpose(0, 2, 4, 1, 3, 5).reshape(nx, ny, nz, 8)
    kinetic = jnp.where(occupied, 0.5 * jnp.sum(velocities * velocities, axis=0), 0.0)
    sub = lax.broadcasted_iota(jnp.int32, (nx, ny, nz, 8, 128), 3)
    lat = jnp.sum(jnp.where(grid_cells[..., None, :] == sub, kinetic[..., None, :], 0.0), axis=-1)
    row = jnp.concatenate([lat, e, jnp.zeros((nx, ny, nz, 112), F32)], axis=-1)
    parked = jnp.where(occupied[None], positions, 1000.0)
    field = jnp.concatenate([parked, row[None]], axis=0)
    field = extend(field, (("gx", 1), ("gz", 3), ("gy", 2)), 2)
    e_new, diff = diffuse_call(field[3])
    heat = e_new[..., :8].reshape(nx, ny, nz, 2, 2, 2).transpose(0, 3, 1, 4, 2, 5)
    heat = heat.reshape(2 * nx, 2 * ny, 2 * nz)
    heat = lax.all_to_all(heat, "gz", split_axis=1, concat_axis=2, tiled=True)
    gidx = jnp.where(occupied, grid_cells, 8)
    velocity_out = main_call(field[:3], velocities, gidx, diff)
    return velocity_out, heat


def solution(mesh):
    return jax.shard_map(
        per_device,
        mesh=mesh,
        in_specs=(
            P(None, "gx", "gy", "gz", None),
            P(None, "gx", "gy", "gz", None),
            P("gx", "gy", "gz"),
            P("gx", "gy", "gz", None),
            P("gx", ("gy", "gz"), None),
        ),
        out_specs=(P(None, "gx", "gy", "gz", None), P("gx", ("gy", "gz"), None)),
        check_vma=False,
    )
```

```python
import functools
import numpy as np
import jax
import jax.numpy as jnp
from jax import lax
from jax.experimental import pallas as pl
from jax.experimental.pallas import tpu as pltpu
from jax.sharding import PartitionSpec as P

CUT = 30.25
EDGE = 11.0
HALF = 5.5
BIG = 10000.0
GROUP = 4
F32 = jnp.float32
BF = jnp.bfloat16
VM = pl.BlockSpec(memory_space=pltpu.VMEM)
SHIFTS = [(x, y, z) for x in (-1, 0, 1) for y in (-1, 0, 1) for z in (-1, 0, 1)]


def split3(v):
    hi = v.astype(BF).astype(F32)
    rest = v - hi
    mid = rest.astype(BF).astype(F32)
    return hi, mid, rest - mid


def shift_tables():
    m = np.zeros((27, 8, 128), np.float32)
    k = np.zeros((27, 8, 128), np.float32)
    for n, o in enumerate(SHIFTS):
        m[n, 0:5] = 1.0
        for a in range(3):
            m[n, 5 + a] = o[a]
            k[n, a] = -2.0 * EDGE * o[a]
            k[n, 4] -= EDGE * EDGE * abs(o[a])
    return jnp.asarray(m), jnp.asarray(k)


def cell_rows(pos_ref, x, y, z):
    px = pos_ref[0, x, y, pl.ds(z, 1), :]
    py = pos_ref[1, x, y, pl.ds(z, 1), :]
    pz = pos_ref[2, x, y, pl.ds(z, 1), :]
    empty = px > 500.0
    qx = jnp.where(empty, 0.0, px - HALF)
    qy = jnp.where(empty, 0.0, py - HALF)
    qz = jnp.where(empty, 0.0, pz - HALF)
    s = jnp.where(empty, BIG, qx * qx + qy * qy + qz * qz)
    return [jnp.broadcast_to(v, (8, 128)) for v in (qx, qy, qz, s)]


def pick(row, *vals):
    out = vals[-1]
    for n in range(len(vals) - 2, -1, -1):
        out = jnp.where(row == n, vals[n], out)
    return out


def neighbour_block(row, rows):
    qx, qy, qz, s = rows
    hi, mid, lo = split3(pick(row, qx, qy, qz, s, jnp.float32(1.0), jnp.float32(2.0 * EDGE)))
    return jnp.concatenate([hi, mid, lo, hi, mid, hi, jnp.zeros_like(hi), jnp.zeros_like(hi)], axis=0)


def centre_block(row, rows):
    qx, qy, qz, s = rows
    return pick(row, 2.0 * qx, 2.0 * qy, 2.0 * qz, jnp.float32(-1.0), CUT - s, qx, qy, qz)


def weights(d, m, k):
    u1, u2, u3 = split3(d * m + k)
    z = jnp.zeros((16, 128), BF)
    c = lambda p, q: jnp.concatenate([p, q], axis=0).astype(BF)
    return jnp.concatenate([c(u1, u1), c(u1, u2), c(u2, u3), z], axis=0)


def dot(a, b):
    return jnp.dot(a, b, preferred_element_type=F32)


def pair_values(table, odd, c0, c1):
    z = jnp.zeros((64, 128), BF)
    left, right = (c0, z), (z, c1)
    if odd:
        left, right = (z, c0), (c1, z)
    rhs = jnp.concatenate([jnp.concatenate(left, 0), jnp.concatenate(right, 0)], 1)
    return jnp.maximum(dot(table, rhs), 0.0)


def same_slot():
    jj = lax.broadcasted_iota(jnp.int32, (128, 256), 0)
    ii = lax.broadcasted_iota(jnp.int32, (128, 256), 1)
    return (jj == ii) | (jj + 128 == ii)


def density_kernel(dims, pos_ref, m_ref, k_ref, sl_ref, te_ref):
    EX, EY, EZ = dims
    NT = EZ - 1
    row = lax.broadcasted_iota(jnp.int32, (8, 128), 0)
    low = lax.broadcasted_iota(jnp.int32, (128, 128), 1) < 64

    def prep(n, carry):
        x = n // EY
        y = n % EY
        tables = []
        for p in range(EZ // 2):
            a = neighbour_block(row, cell_rows(pos_ref, x, y, 2 * p))
            b = neighbour_block(row, cell_rows(pos_ref, x, y, 2 * p + 1))
            tables.append(jnp.concatenate([a, b], 0).T)
        for layer in range(NT):
            p = layer // 2
            t = tables[p] if layer % 2 == 0 else jnp.where(low, tables[p + 1], tables[p])
            te_ref[n * NT + layer] = t.astype(BF)
        return carry

    lax.fori_loop(0, EX * EY, prep, 0)
    sl_ref[...] = jnp.zeros(sl_ref.shape, F32)
    diag = same_slot()
    DY = EY - 2
    DP = (EZ - 2) // 2

    def dens(n, carry):
        y = n % DY + 1
        x = n // DY + 1
        centres = [centre_block(row, cell_rows(pos_ref, x, y, z)) for z in range(1, EZ - 1)]
        acc = [jnp.zeros((8, 256), F32) for _ in range(DP)]
        for n_shift, (ox, oy, oz) in enumerate(SHIFTS):
            m, k = m_ref[n_shift], k_ref[n_shift]
            base = ((x + ox) * EY + y + oy) * NT + oz
            for p in range(DP):
                z0 = 1 + 2 * p
                c0, c1 = [weights(d, m, k) for d in centres[2 * p:2 * p + 2]]
                r = pair_values(te_ref[base + z0], oz == 0, c0, c1)
                if n_shift == 13:
                    r = jnp.where(diag, 0.0, r)
                w = r * r * r
                acc[p] = acc[p] + w.reshape(16, 8, 256).sum(0)
        for p in range(DP):
            d = jnp.sum(acc[p], axis=0, keepdims=True) * (1.0 / CUT ** 3)
            sl = -0.5 / jnp.sqrt(d + 1.0)
            sl_ref[x - 1, y, pl.ds(1 + 2 * p, 1), :] = sl[:, :128]
            sl_ref[x - 1, y, pl.ds(2 + 2 * p, 1), :] = sl[:, 128:]
        return carry

    lax.fori_loop(0, (EX - 2) * DY, dens, 0)


def density_call(pos):
    EX, EY, EZ = pos.shape[1:4]
    m, k = shift_tables()
    return pl.pallas_call(
        functools.partial(density_kernel, (EX, EY, EZ)),
        out_shape=(
            jax.ShapeDtypeStruct((EX - 2, EY, EZ, 128), F32),
            jax.ShapeDtypeStruct((EX * EY * (EZ - 1), 128, 128), BF),
        ),
        in_specs=[VM] * 3,
        out_specs=(VM, VM),
        compiler_params=pltpu.CompilerParams(vmem_limit_bytes=24 * 2 ** 20),
        name="density",
    )(pos, m, k)


def force_kernel(dims, pos_ref, te_ref, sl_ref, vel_ref, grid_ref, diff_ref, m_ref, k_ref, out_ref, g_ref):
    EX, EY, EZ = dims
    NT = EZ - 1
    GY, GZ = EY - 2, EZ - 2
    row = lax.broadcasted_iota(jnp.int32, (8, 128), 0)
    diag = same_slot()

    def gprep(n, carry):
        x = n // GY
        y = n % GY + 1
        for z in range(1, EZ - 1):
            qx, qy, qz, _ = cell_rows(pos_ref, x, y, z)
            s = jnp.broadcast_to(sl_ref[x, y, pl.ds(z, 1), :], (8, 128))
            v = pick(row % 4, qx, qy, qz, jnp.ones_like(qx))
            hi, mid, lo = split3(v * jnp.where(row < 4, 1.0, s))
            g_ref[n * GZ + z - 1] = jnp.concatenate([hi, mid, lo, jnp.zeros_like(hi)], 0).astype(BF)
        return carry

    lax.fori_loop(0, EX * GY, gprep, 0)
    FY = EY - 4

    def force(n, carry):
        x = n // (FY // GROUP) + 1
        first = n % (FY // GROUP) * GROUP + 2
        z0 = 2
        rows = [[cell_rows(pos_ref, x, first + c, z0 + h) for h in range(2)] for c in range(GROUP)]
        centres = [[centre_block(row, r) for r in pair] for pair in rows]
        zero = jnp.zeros((8, 128), F32)
        acc = [[[zero] * 4, [zero] * 4] for c in range(GROUP)]
        for n_shift, shift in enumerate(SHIFTS):
            ox, oy, oz = shift
            m, k = m_ref[n_shift], k_ref[n_shift]
            layer = z0 + oz
            for c in range(GROUP):
                y = first + c
                base = ((x + ox) * EY + y + oy) * NT + layer
                c0, c1 = [weights(d, m, k) for d in centres[c]]
                r = pair_values(te_ref[base], layer % 2 == 1, c0, c1)
                if n_shift == 13:
                    r = jnp.where(diag, 0.0, r)
                t = r * r
                hi = t.astype(BF)
                lo = (t - hi.astype(F32)).astype(BF)
                gbase = ((x + ox) * GY + y + oy - 1) * GZ + layer - 1
                for h in range(2):
                    ls = slice(128 * h, 128 * h + 128)
                    tt = jnp.concatenate([hi[:, ls], lo[:, ls]], 0)
                    g = g_ref[gbase + h]
                    f = dot(jnp.concatenate([g, g], 1), tt)
                    f = f[0:8] + f[8:16] + f[16:24]
                    total = acc[c][h]
                    total[0] = total[0] + f
                    for a in range(3):
                        if shift[a] == 1:
                            total[a + 1] = total[a + 1] + f
                        elif shift[a] == -1:
                            total[a + 1] = total[a + 1] - f
        for c, h in [(c, h) for c in range(GROUP) for h in range(2)]:
            y = first + c
            total = acc[c][h]
            s = sl_ref[x, y, pl.ds(z0 + h, 1), :]
            sub = grid_ref[x - 1, y - 2, pl.ds(h, 1), :]
            both = diff_ref[pl.ds(y * EZ + z0 + h, 1), :]
            here = jnp.where(x == 1, both[:, 16:24], both[:, 24:32])
            heat = jnp.zeros((1, 128), F32)
            for kk in range(8):
                heat = jnp.where(sub == kk, here[:, kk:kk + 1], heat)
            for a in range(3):
                q = rows[c][h][a][0:1]
                plain = total[0][a:a + 1] + EDGE * total[1 + a][3:4] - q * total[0][3:4]
                sloped = total[0][4 + a:5 + a] + EDGE * total[1 + a][7:8] - q * total[0][7:8]
                f = (2.0 / CUT ** 2) * ((-3.0 / CUT) * (s * plain + sloped) + (-1.5 / CUT) * plain)
                v = vel_ref[a, x - 1, y - 2, pl.ds(h, 1), :]
                moved = v + 0.2 * f + 0.02 * heat * v
                out_ref[a, x - 1, y - 2, pl.ds(h, 1), :] = jnp.where(sub < 8, moved, 0.0)
        return carry

    lax.fori_loop(0, (EX - 2) * FY // GROUP, force, 0)


def force_call(pos, te, slopes, vel, sub, diff):
    EX, EY, EZ = pos.shape[1:4]
    m, k = shift_tables()
    return pl.pallas_call(
        functools.partial(force_kernel, (EX, EY, EZ)),
        out_shape=jax.ShapeDtypeStruct(vel.shape, F32),
        in_specs=[VM] * 8,
        out_specs=VM,
        scratch_shapes=[pltpu.VMEM((EX * (EY - 2) * (EZ - 2), 32, 128), BF)],
        compiler_params=pltpu.CompilerParams(vmem_limit_bytes=24 * 2 ** 20),
        name="force",
    )(pos, te, slopes, vel, sub, diff, m, k)


def diffuse_kernel(EZ, x_ref, e_out, diff_out, e_ref):
    rows = x_ref.shape[0]
    own = x_ref[...]
    lane = lax.broadcasted_iota(jnp.int32, (rows, 128), 1)
    lat = pltpu.roll(own, 64, 1)
    e = own
    e_ref[...] = jnp.zeros(e_ref.shape, F32)
    for step in range(4):
        e_ref[pl.ds(8, rows), :] = e
        beside = pltpu.roll(e, 4, 1) + pltpu.roll(e, 124, 1)
        for bit, stride in ((1, 1), (2, EZ)):
            after = e_ref[pl.ds(8 + stride, rows), :]
            before = e_ref[pl.ds(8 - stride, rows), :]
            low = pltpu.roll(e + before, 128 - bit, 1)
            high = pltpu.roll(e + after, bit, 1)
            beside = beside + jnp.where((lane & bit) == 0, low, high)
        e = e + 0.15 * (beside - 6.0 * e) - 0.05 * (e - lat)
    e_out[...] = e
    diff_out[...] = e - lat


def diffuse_call(grid):
    EY, EZ = grid.shape[:2]
    rows = EY * EZ
    shape = jax.ShapeDtypeStruct((rows, 128), F32)
    return pl.pallas_call(
        functools.partial(diffuse_kernel, EZ),
        out_shape=(shape, shape),
        in_specs=[VM],
        out_specs=(VM, VM),
        scratch_shapes=[pltpu.VMEM((rows + 16, 128), F32)],
        name="diffusion",
    )(grid.reshape(rows, 128))


def ring(value, axis, step):
    n = lax.axis_size(axis)
    return lax.ppermute(value, axis, [(i, (i + step) % n) for i in range(n)])


def around(value, axis, dim, width):
    length = value.shape[dim]
    before = ring(lax.slice_in_dim(value, length - width, length, axis=dim), axis, 1)
    after = ring(lax.slice_in_dim(value, 0, width, axis=dim), axis, -1)
    return before, after


def per_device(positions, velocities, counts, grid_cells, electron_temp):
    nx, ny, nz = counts.shape
    slot = lax.broadcasted_iota(jnp.int32, grid_cells.shape, 3)
    occupied = slot < counts[..., None]
    blocks = electron_temp.reshape(2 * nx, 1, -1, 4)
    wide = jnp.concatenate([jnp.roll(blocks, 1, 2), blocks, jnp.roll(blocks, -1, 2)], -1)
    wide = wide.reshape(2 * nx, 1, -1)
    e = lax.all_to_all(wide, "gz", split_axis=2, concat_axis=1, tiled=True)
    e = e.reshape(2 * nx, ny, 2, 6, 2).transpose(1, 3, 0, 2, 4).reshape(ny, 6, 8 * nx)
    kinetic = jnp.where(occupied, 0.5 * jnp.sum(velocities * velocities, axis=0), 0.0)
    sub = lax.broadcasted_iota(jnp.int32, (nx, ny, nz, 8, 128), 3)
    lat = jnp.sum(jnp.where(grid_cells[..., None, :] == sub, kinetic[..., None, :], 0.0), axis=-1)
    lat = lat.transpose(1, 2, 0, 3).reshape(1, ny, nz, 8 * nx)
    lat = jnp.pad(lat, ((0, 0), (0, 0), (0, 0), (0, 128 - 8 * nx)))
    parked = jnp.where(occupied[None], positions, 1000.0).reshape(3 * nx, ny, nz, 128)
    planes = jnp.concatenate([parked, lat], 0)
    before, after = around(planes, "gz", 2, 2)
    planes = jnp.concatenate([before, planes, after], 2)
    pos = planes[:3 * nx].reshape(3, nx, ny, 6, 128)
    field = jnp.concatenate([planes[3 * nx, ..., :8 * nx], e], -1)
    field = jnp.pad(field, ((0, 0), (0, 0), (0, 128 - 16 * nx)))[None]
    before = ring(jnp.concatenate([pos[:, -1], field], 0), "gx", 1)
    after = ring(jnp.concatenate([pos[:, 0], field], 0), "gx", -1)
    pos = jnp.concatenate([before[:3, None], pos, after[:3, None]], 1)
    three = [before[3], field[0], after[3]]
    gap = jnp.zeros((ny, 6, 64 - 24 * nx), F32)
    w = 8 * nx
    row = jnp.concatenate([t[..., w:2 * w] for t in three] + [gap] + [t[..., :w] for t in three] + [gap], -1)
    planes = jnp.concatenate([pos.reshape(3 * nx + 6, ny, 6, 128), row[None]], 0)
    before, after = around(planes, "gy", 1, 2)
    planes = jnp.concatenate([before, planes, after], 1)
    pos = planes[:-1].reshape(3, nx + 2, ny + 4, 6, 128)
    e_new, diff = diffuse_call(planes[-1])
    slopes, te = density_call(pos)
    s_before, s_after = around(slopes, "gx", 0, 1)
    slopes = jnp.concatenate([s_before, slopes, s_after], 0)
    heat = e_new.reshape(ny + 4, 6, 128)[2:-2, 2:-2, w:2 * w].reshape(ny, nz, 2 * nx, 2, 2)
    heat = heat.transpose(2, 0, 3, 1, 4).reshape(2 * nx, 2 * ny, 2 * nz)
    heat = lax.all_to_all(heat, "gz", split_axis=1, concat_axis=2, tiled=True)
    velocity_out = force_call(pos, te, slopes, velocities, jnp.where(occupied, grid_cells, 8), diff)
    return velocity_out, heat


def solution(mesh):
    return jax.shard_map(
        per_device,
        mesh=mesh,
        in_specs=(
            P(None, "gx", "gy", "gz", None),
            P(None, "gx", "gy", "gz", None),
            P("gx", "gy", "gz"),
            P("gx", "gy", "gz", None),
            P("gx", ("gy", "gz"), None),
        ),
        out_specs=(P(None, "gx", "gy", "gz", None), P("gx", ("gy", "gz"), None)),
        check_vma=False,
    )
```

```python
import functools
import numpy as np
import jax
import jax.numpy as jnp
from jax import lax
from jax.experimental import pallas as pl
from jax.experimental.pallas import tpu as pltpu
from jax.sharding import PartitionSpec as P

CUT = 30.25
EDGE = 11.0
HALF = 5.5
BIG = 10000.0
GROUP = 4
F32 = jnp.float32
BF = jnp.bfloat16
VM = pl.BlockSpec(memory_space=pltpu.VMEM)
SHIFTS = [(x, y, z) for x in (-1, 0, 1) for y in (-1, 0, 1) for z in (-1, 0, 1)]


def split3(v):
    hi = v.astype(BF).astype(F32)
    rest = v - hi
    mid = rest.astype(BF).astype(F32)
    return hi, mid, rest - mid


def shift_tables():
    m = np.zeros((27, 8, 128), np.float32)
    k = np.zeros((27, 8, 128), np.float32)
    for n, o in enumerate(SHIFTS):
        m[n, 0:5] = 1.0
        for a in range(3):
            m[n, 5 + a] = o[a]
            k[n, a] = -2.0 * EDGE * o[a]
            k[n, 4] -= EDGE * EDGE * abs(o[a])
    return jnp.asarray(m), jnp.asarray(k)


def cell_rows(pos_ref, x, y, z):
    px = pos_ref[x, y, pl.ds(z, 1), :]
    py = pos_ref[4 + x, y, pl.ds(z, 1), :]
    pz = pos_ref[8 + x, y, pl.ds(z, 1), :]
    empty = px > 500.0
    qx = jnp.where(empty, 0.0, px - HALF)
    qy = jnp.where(empty, 0.0, py - HALF)
    qz = jnp.where(empty, 0.0, pz - HALF)
    s = jnp.where(empty, BIG, qx * qx + qy * qy + qz * qz)
    return [jnp.broadcast_to(v, (8, 128)) for v in (qx, qy, qz, s)]


def pick(row, *vals):
    out = vals[-1]
    for n in range(len(vals) - 2, -1, -1):
        out = jnp.where(row == n, vals[n], out)
    return out


def neighbour_block(row, rows):
    qx, qy, qz, s = rows
    hi, mid, lo = split3(pick(row, qx, qy, qz, s, jnp.float32(1.0), jnp.float32(2.0 * EDGE)))
    return jnp.concatenate([hi, mid, lo, hi, mid, hi, jnp.zeros_like(hi), jnp.zeros_like(hi)], axis=0)


def centre_block(row, rows):
    qx, qy, qz, s = rows
    return pick(row, 2.0 * qx, 2.0 * qy, 2.0 * qz, jnp.float32(-1.0), CUT - s, qx, qy, qz)


def weights(d, m, k):
    u1, u2, u3 = split3(d * m + k)
    z = jnp.zeros((16, 128), BF)
    c = lambda p, q: jnp.concatenate([p, q], axis=0).astype(BF)
    return jnp.concatenate([c(u1, u1), c(u1, u2), c(u2, u3), z], axis=0)


def dot(a, b):
    return jnp.dot(a, b, preferred_element_type=F32)


def pair_values(table, c0, c1):
    z = jnp.zeros((64, 128), BF)
    rhs = jnp.concatenate([jnp.concatenate([c0, z], 0), jnp.concatenate([z, c1], 0)], 1)
    return jnp.maximum(dot(table, rhs), 0.0)


def same_slot():
    return lax.broadcasted_iota(jnp.int32, (128, 128), 0) == lax.broadcasted_iota(jnp.int32, (128, 128), 1)


TABLES = ((0, 1), (2, 1), (2, 3))
DENSITY_TILES = ((0, 0, 1), (0, 1, 0), (1, 1, 2), (2, 2, 3), (2, 3, 2))
FORCE_TILES = ((0, 1, 1), (1, 1, 2), (2, 2, 2))


def main_kernel(own_ref, xb_ref, xa_ref, yb_ref, ya_ref, vel_ref, sub_ref, diff_ref, m_ref, k_ref,
                out_ref, pos_ref, te_ref, cen_ref, sl_ref, g_ref):
    NX, NY = 4, 10
    row = lax.broadcasted_iota(jnp.int32, (8, 128), 0)
    low = lax.broadcasted_iota(jnp.int32, (128, 128), 1) < 64
    diag = same_slot()
    for a in range(3):
        pos_ref[4 * a, 1:9] = xb_ref[a]
        pos_ref[4 * a + 1, 1:9] = own_ref[2 * a]
        pos_ref[4 * a + 2, 1:9] = own_ref[2 * a + 1]
        pos_ref[4 * a + 3, 1:9] = xa_ref[a]
    pos_ref[:, 0] = yb_ref[0:12]
    pos_ref[:, 9] = ya_ref[0:12]

    def prep(n, carry):
        x = n // NY
        y = n % NY
        blocks = []
        for z in range(4):
            rows = cell_rows(pos_ref, x, y, z + 1)
            blocks.append(neighbour_block(row, rows))
            cen_ref[(x * NY + y) * 4 + z] = centre_block(row, rows)
        a = jnp.concatenate(blocks[:2], 0).T
        b = jnp.concatenate(blocks[2:], 0).T
        base = (x * (NY + 2) + y + 1) * 3
        te_ref[base] = a.astype(BF)
        te_ref[base + 1] = jnp.where(low, b, a).astype(BF)
        te_ref[base + 2] = b.astype(BF)
        return carry

    lax.fori_loop(0, NX * NY, prep, 0)
    for x in range(NX):
        for y in (0, NY + 1):
            te_ref[pl.ds((x * (NY + 2) + y) * 3, 3)] = jnp.zeros((3, 128, 128), BF)

    def dens(y, carry):
        for x in range(NX):
            centres = [cen_ref[(x * NY + y) * 4 + z] for z in range(4)]
            acc = [jnp.zeros((8, 128), F32) for z in range(4)]
            for ox in (-1, 0, 1):
                if not 0 <= x + ox < NX:
                    continue
                for oy in (-1, 0, 1):
                    base = ((x + ox) * (NY + 2) + y + 1 + oy) * 3
                    for t, ca, cb in DENSITY_TILES:
                        w = []
                        for half, c in ((0, ca), (1, cb)):
                            o = SHIFTS.index((ox, oy, TABLES[t][half] - c))
                            w.append(weights(centres[c], m_ref[o], k_ref[o]))
                        r = pair_values(te_ref[base + t], *w)
                        r3 = r * r * r
                        for half, c in ((0, ca), (1, cb)):
                            part = r3[:, 128 * half:128 * half + 128]
                            if (ox, oy) == (0, 0) and TABLES[t][half] == c:
                                part = jnp.where(diag, 0.0, part)
                            acc[c] = acc[c] + part.reshape(16, 8, 128).sum(0)
            for z in range(4):
                d = jnp.sum(acc[z], axis=0, keepdims=True) * (1.0 / CUT ** 3)
                sl_ref[x, y, pl.ds(z, 1), :] = -0.5 / jnp.sqrt(d + 1.0)
        return carry

    lax.fori_loop(0, NY, dens, 0)

    def gprep(n, carry):
        x = n // NY
        y = n % NY
        for z in range(4):
            qx, qy, qz, _ = cell_rows(pos_ref, x, y, z + 1)
            s = jnp.broadcast_to(sl_ref[x, y, pl.ds(z, 1), :], (8, 128))
            v = pick(row % 4, qx, qy, qz, jnp.ones_like(qx))
            hi, mid, lo = split3(v * jnp.where(row < 4, 1.0, s))
            g_ref[n * 4 + z] = jnp.concatenate([hi, mid, lo, jnp.zeros_like(hi)], 0).astype(BF)
        return carry

    lax.fori_loop(0, NX * NY, gprep, 0)

    def force(n, carry):
        x = n // (8 // GROUP) + 1
        first = n % (8 // GROUP) * GROUP + 1
        zero = jnp.zeros((8, 128), F32)
        acc = [[[zero] * 4, [zero] * 4] for c in range(GROUP)]
        for ox in (-1, 0, 1):
            for oy in (-1, 0, 1):
                for c in range(GROUP):
                    y = first + c
                    col = (x + ox) * NY + y + oy
                    base = ((x + ox) * (NY + 2) + y + 1 + oy) * 3
                    for t, ca, cb in FORCE_TILES:
                        w = []
                        for half, z in ((0, ca), (1, cb)):
                            o = SHIFTS.index((ox, oy, TABLES[t][half] - z))
                            w.append(weights(cen_ref[(x * NY + y) * 4 + z], m_ref[o], k_ref[o]))
                        r = pair_values(te_ref[base + t], *w)
                        for half, z in ((0, ca), (1, cb)):
                            layer = TABLES[t][half]
                            shift = (ox, oy, layer - z)
                            p = r[:, 128 * half:128 * half + 128]
                            if shift == (0, 0, 0):
                                p = jnp.where(diag, 0.0, p)
                            p = p * p
                            hi = p.astype(BF)
                            lo = (p - hi.astype(F32)).astype(BF)
                            g = g_ref[col * 4 + layer]
                            f = dot(jnp.concatenate([g, g], 1), jnp.concatenate([hi, lo], 0))
                            f = f[0:8] + f[8:16] + f[16:24]
                            total = acc[c][z - 1]
                            total[0] = total[0] + f
                            for a in range(3):
                                if shift[a] == 1:
                                    total[a + 1] = total[a + 1] + f
                                elif shift[a] == -1:
                                    total[a + 1] = total[a + 1] - f
        for c, h in [(c, h) for c in range(GROUP) for h in range(2)]:
            y = first + c
            total = acc[c][h]
            rows = cell_rows(pos_ref, x, y, h + 2)
            s = sl_ref[x, y, pl.ds(h + 1, 1), :]
            sub = sub_ref[x - 1, y - 1, pl.ds(h, 1), :]
            both = diff_ref[pl.ds((y + 1) * 6 + 2 + h, 1), :]
            here = jnp.where(x == 1, both[:, 16:24], both[:, 24:32])
            heat = jnp.zeros((1, 128), F32)
            for kk in range(8):
                heat = jnp.where(sub == kk, here[:, kk:kk + 1], heat)
            for a in range(3):
                q = rows[a][0:1]
                plain = total[0][a:a + 1] + EDGE * total[1 + a][3:4] - q * total[0][3:4]
                sloped = total[0][4 + a:5 + a] + EDGE * total[1 + a][7:8] - q * total[0][7:8]
                f = (2.0 / CUT ** 2) * ((-3.0 / CUT) * (s * plain + sloped) + (-1.5 / CUT) * plain)
                v = vel_ref[a, x - 1, y - 1, pl.ds(h, 1), :]
                moved = v + 0.2 * f + 0.02 * heat * v
                out_ref[a, x - 1, y - 1, pl.ds(h, 1), :] = jnp.where(sub < 8, moved, 0.0)
        return carry

    lax.fori_loop(0, 16 // GROUP, force, 0)


def main_call(own, xb, xa, yb, ya, vel, sub, diff):
    m, k = shift_tables()
    return pl.pallas_call(
        main_kernel,
        out_shape=jax.ShapeDtypeStruct(vel.shape, F32),
        in_specs=[VM] * 10,
        out_specs=VM,
        scratch_shapes=[
            pltpu.VMEM((12, 10, 6, 128), F32),
            pltpu.VMEM((4 * 12 * 3, 128, 128), BF),
            pltpu.VMEM((160, 8, 128), F32),
            pltpu.VMEM((4, 10, 4, 128), F32),
            pltpu.VMEM((160, 32, 128), BF),
        ],
        compiler_params=pltpu.CompilerParams(vmem_limit_bytes=24 * 2 ** 20),
        name="pair_forces",
    )(own, xb, xa, yb, ya, vel, sub, diff, m, k)


def pack_kernel(own_ref, e_ref, xb_ref, xa_ref, up_ref, down_ref, mid_ref):
    lane = lax.broadcasted_iota(jnp.int32, (6, 128), 1)
    for y in range(8):
        lat = own_ref[6, y]
        mine = e_ref[y]
        e_part = jnp.where(lane < 16, pltpu.roll(xb_ref[3, y], 112, 1),
                           jnp.where(lane < 32, mine, pltpu.roll(xa_ref[3, y], 16, 1)))
        l_part = jnp.where(lane < 80, pltpu.roll(xb_ref[3, y], 64, 1),
                           jnp.where(lane < 96, pltpu.roll(lat, 80, 1), pltpu.roll(xa_ref[3, y], 96, 1)))
        used = (lane < 48) | ((lane >= 64) & (lane < 112))
        mid_ref[y] = jnp.where(used, jnp.where(lane < 64, e_part, l_part), 0.0)
    for ref, y in ((up_ref, 7), (down_ref, 0)):
        for a in range(3):
            ref[4 * a] = xb_ref[a, y]
            ref[4 * a + 1] = own_ref[2 * a, y]
            ref[4 * a + 2] = own_ref[2 * a + 1, y]
            ref[4 * a + 3] = xa_ref[a, y]
        for n in range(2):
            ref[12 + n] = mid_ref[(y // 7) * 6 + n]


def pack_call(own, e, xb, xa):
    message = jax.ShapeDtypeStruct((14, 6, 128), F32)
    return pl.pallas_call(
        pack_kernel,
        out_shape=(message, message, jax.ShapeDtypeStruct((8, 6, 128), F32)),
        in_specs=[VM] * 4,
        out_specs=(VM, VM, VM),
        compiler_params=pltpu.CompilerParams(vmem_limit_bytes=2 * 2 ** 20),
        name="pack",
    )(own, e, xb, xa)


def diffuse_kernel(mid_ref, yb_ref, ya_ref, e_out, diff_out, x_ref, e_ref):
    for n in range(2):
        x_ref[pl.ds(6 * n, 6)] = yb_ref[12 + n]
        x_ref[pl.ds(60 + 6 * n, 6)] = ya_ref[12 + n]
    for y in range(8):
        x_ref[pl.ds(12 + 6 * y, 6)] = mid_ref[y]
    rows = 72
    own = x_ref[...]
    lane = lax.broadcasted_iota(jnp.int32, (rows, 128), 1)
    lat = pltpu.roll(own, 64, 1)
    e = own
    e_ref[...] = jnp.zeros(e_ref.shape, F32)
    for step in range(4):
        e_ref[pl.ds(8, rows), :] = e
        beside = pltpu.roll(e, 4, 1) + pltpu.roll(e, 124, 1)
        for bit, stride in ((1, 1), (2, 6)):
            after = e_ref[pl.ds(8 + stride, rows), :]
            before = e_ref[pl.ds(8 - stride, rows), :]
            low = pltpu.roll(e + before, 128 - bit, 1)
            high = pltpu.roll(e + after, bit, 1)
            beside = beside + jnp.where((lane & bit) == 0, low, high)
        e = e + 0.15 * (beside - 6.0 * e) - 0.05 * (e - lat)
    e_ref[pl.ds(8, rows), :] = e
    for y in range(8):
        e_out[y] = e_ref[pl.ds(8 + 6 * (y + 2) + 2, 2), :]
    diff_out[...] = e - lat


def diffuse_call(mid, yb, ya):
    return pl.pallas_call(
        diffuse_kernel,
        out_shape=(jax.ShapeDtypeStruct((8, 2, 128), F32), jax.ShapeDtypeStruct((72, 128), F32)),
        in_specs=[VM] * 3,
        out_specs=(VM, VM),
        scratch_shapes=[pltpu.VMEM((72, 128), F32), pltpu.VMEM((88, 128), F32)],
        compiler_params=pltpu.CompilerParams(vmem_limit_bytes=2 * 2 ** 20),
        name="diffusion",
    )(mid, yb, ya)


def ring(value, axis, step):
    n = lax.axis_size(axis)
    return lax.ppermute(value, axis, [(i, (i + step) % n) for i in range(n)])


def per_device(positions, velocities, counts, grid_cells, electron_temp):
    nx, ny, nz = counts.shape
    slot = lax.broadcasted_iota(jnp.int32, grid_cells.shape, 3)
    occupied = slot < counts[..., None]
    shifted = [jnp.roll(electron_temp, 4, 2), electron_temp, jnp.roll(electron_temp, -4, 2)]
    e = lax.all_to_all(jnp.concatenate(shifted, 0), "gz", split_axis=2, concat_axis=1, tiled=True)
    e = e.reshape(3, 4, ny, 2, nz, 2).transpose(2, 0, 4, 1, 3, 5).reshape(ny, 6, 16)
    e = jnp.pad(e, ((0, 0), (0, 0), (16, 96)))
    kinetic = jnp.where(occupied, 0.5 * jnp.sum(velocities * velocities, axis=0), 0.0)
    sub = lax.broadcasted_iota(jnp.int32, (nx, ny, nz, 8, 128), 3)
    lat = jnp.sum(jnp.where(grid_cells[..., None, :] == sub, kinetic[..., None, :], 0.0), axis=-1)
    lat = lat.transpose(1, 2, 0, 3).reshape(1, ny, nz, 16)
    lat = jnp.pad(lat, ((0, 0), (0, 0), (0, 0), (0, 112)))
    parked = jnp.where(occupied[None], positions, 1000.0).reshape(6, ny, nz, 128)
    planes = jnp.concatenate([parked, lat], 0)
    own = jnp.concatenate([ring(planes, "gz", 1), planes, ring(planes, "gz", -1)], 2)
    field = (own[6] + e)[None]
    xb = ring(jnp.concatenate([own[1:6:2], field], 0), "gx", 1)
    xa = ring(jnp.concatenate([own[0:6:2], field], 0), "gx", -1)
    up, down, mid = pack_call(own, e, xb, xa)
    yb = ring(up, "gy", 1)
    ya = ring(down, "gy", -1)
    e_new, diff = diffuse_call(mid, yb, ya)
    heat = e_new[..., 16:32].reshape(ny, nz, 4, 2, 2).transpose(2, 0, 3, 1, 4).reshape(4, 2 * ny, 2 * nz)
    heat = lax.all_to_all(heat, "gz", split_axis=1, concat_axis=2, tiled=True)
    vel_out = main_call(own, xb, xa, yb, ya, velocities, jnp.where(occupied, grid_cells, 8), diff)
    return vel_out, heat


def solution(mesh):
    return jax.shard_map(
        per_device,
        mesh=mesh,
        in_specs=(
            P(None, "gx", "gy", "gz", None),
            P(None, "gx", "gy", "gz", None),
            P("gx", "gy", "gz"),
            P("gx", "gy", "gz", None),
            P("gx", ("gy", "gz"), None),
        ),
        out_specs=(P(None, "gx", "gy", "gz", None), P("gx", ("gy", "gz"), None)),
        check_vma=False,
    )
```

```python
import functools
import numpy as np
import jax
import jax.numpy as jnp
from jax import lax
from jax.experimental import pallas as pl
from jax.experimental.pallas import tpu as pltpu
from jax.sharding import PartitionSpec as P

CUT = 30.25
EDGE = 11.0
HALF = 5.5
BIG = 10000.0
GROUP = 4
F32 = jnp.float32
BF = jnp.bfloat16
VM = pl.BlockSpec(memory_space=pltpu.VMEM)
SHIFTS = [(x, y, z) for x in (-1, 0, 1) for y in (-1, 0, 1) for z in (-1, 0, 1)]


def split3(v):
    hi = v.astype(BF).astype(F32)
    rest = v - hi
    mid = rest.astype(BF).astype(F32)
    return hi, mid, rest - mid


def shift_tables():
    m = np.zeros((27, 8, 128), np.float32)
    k = np.zeros((27, 8, 128), np.float32)
    for n, o in enumerate(SHIFTS):
        m[n, 0:5] = 1.0
        for a in range(3):
            m[n, 5 + a] = o[a]
            k[n, a] = -2.0 * EDGE * o[a]
            k[n, 4] -= EDGE * EDGE * abs(o[a])
    return jnp.asarray(m), jnp.asarray(k)


def cell_rows(pos_ref, x, y, z):
    px = pos_ref[x, y, pl.ds(z, 1), :]
    py = pos_ref[4 + x, y, pl.ds(z, 1), :]
    pz = pos_ref[8 + x, y, pl.ds(z, 1), :]
    empty = px > 500.0
    qx = jnp.where(empty, 0.0, px - HALF)
    qy = jnp.where(empty, 0.0, py - HALF)
    qz = jnp.where(empty, 0.0, pz - HALF)
    s = jnp.where(empty, BIG, qx * qx + qy * qy + qz * qz)
    return [jnp.broadcast_to(v, (8, 128)) for v in (qx, qy, qz, s)]


def pick(row, *vals):
    out = vals[-1]
    for n in range(len(vals) - 2, -1, -1):
        out = jnp.where(row == n, vals[n], out)
    return out


def neighbour_block(row, rows):
    qx, qy, qz, s = rows
    hi, mid, lo = split3(pick(row, qx, qy, qz, s, jnp.float32(1.0), jnp.float32(2.0 * EDGE)))
    return jnp.concatenate([hi, mid, lo, hi, mid, hi, jnp.zeros_like(hi), jnp.zeros_like(hi)], axis=0)


def centre_block(row, rows):
    qx, qy, qz, s = rows
    return pick(row, 2.0 * qx, 2.0 * qy, 2.0 * qz, jnp.float32(-1.0), CUT - s, qx, qy, qz)


def weights(d, m, k):
    u1, u2, u3 = split3(d * m + k)
    z = jnp.zeros((16, 128), BF)
    c = lambda p, q: jnp.concatenate([p, q], axis=0).astype(BF)
    return jnp.concatenate([c(u1, u1), c(u1, u2), c(u2, u3), z], axis=0)


def dot(a, b):
    return jnp.dot(a, b, preferred_element_type=F32)


def pair_values(table, c0, c1):
    z = jnp.zeros((64, 128), BF)
    rhs = jnp.concatenate([jnp.concatenate([c0, z], 0), jnp.concatenate([z, c1], 0)], 1)
    return jnp.maximum(dot(table, rhs), 0.0)


def same_slot():
    return lax.broadcasted_iota(jnp.int32, (128, 128), 0) == lax.broadcasted_iota(jnp.int32, (128, 128), 1)


TABLES = ((0, 1), (2, 1), (2, 3))
DENSITY_TILES = ((0, 0, 1), (0, 1, 0), (1, 1, 2), (2, 2, 3), (2, 3, 2))
OWN_TILES = ((0, 0, 1), (2, 2, 3), (1, 1, 0), (2, None, 2))
FORCE_TILES = ((0, 1, 1), (1, 1, 2), (2, 2, 2))


def main_kernel(own_ref, xb_ref, xa_ref, yb_ref, ya_ref, vel_ref, sub_ref, diff_ref, m_ref, k_ref,
                out_ref, pos_ref, te_ref, cen_ref, sl_ref, g_ref, row_ref, col_ref):
    NX, NY = 4, 10
    row = lax.broadcasted_iota(jnp.int32, (8, 128), 0)
    low = lax.broadcasted_iota(jnp.int32, (128, 128), 1) < 64
    diag = same_slot()
    for a in range(3):
        pos_ref[4 * a, 1:9] = xb_ref[a]
        pos_ref[4 * a + 1, 1:9] = own_ref[2 * a]
        pos_ref[4 * a + 2, 1:9] = own_ref[2 * a + 1]
        pos_ref[4 * a + 3, 1:9] = xa_ref[a]
    pos_ref[:, 0] = yb_ref[0:12]
    pos_ref[:, 9] = ya_ref[0:12]

    def prep(y, carry):
        for x in range(NX):
            blocks = []
            for z in range(4):
                rows = cell_rows(pos_ref, x, y, z + 1)
                blocks.append(neighbour_block(row, rows))
                cen_ref[(x * NY + y) * 4 + z] = centre_block(row, rows)
            a = jnp.concatenate(blocks[:2], 0).T
            b = jnp.concatenate(blocks[2:], 0).T
            base = (x * (NY + 2) + y + 1) * 3
            te_ref[base] = a.astype(BF)
            te_ref[base + 1] = jnp.where(low, b, a).astype(BF)
            te_ref[base + 2] = b.astype(BF)
        return carry

    lax.fori_loop(0, NY, prep, 0)
    for x in range(NX):
        for y in (0, NY + 1):
            te_ref[pl.ds((x * (NY + 2) + y) * 3, 3)] = jnp.zeros((3, 128, 128), BF)

    row_ref[...] = jnp.zeros(row_ref.shape, F32)

    def dens(y, carry):
        for x in range(NX):
            centres = [cen_ref[(x * NY + y) * 4 + z] for z in range(4)]
            acc = [jnp.zeros((8, 128), F32) for z in range(4)]
            for ox, oy in ((0, 0), (0, 1), (1, -1), (1, 0), (1, 1)):
                if x + ox >= NX:
                    continue
                col = (x + ox) * (NY + 2) + y + 1 + oy
                tiles = OWN_TILES if (ox, oy) == (0, 0) else DENSITY_TILES
                for t, ca, cb in tiles:
                    w = []
                    for half, c in ((0, ca), (1, cb)):
                        if c is None:
                            w.append(jnp.zeros((64, 128), BF))
                            continue
                        o = SHIFTS.index((ox, oy, TABLES[t][half] - c))
                        w.append(weights(centres[c], m_ref[o], k_ref[o]))
                    r = pair_values(te_ref[col * 3 + t], *w)
                    r3 = r * r * r
                    for half, c in ((0, ca), (1, cb)):
                        if c is None:
                            continue
                        layer = TABLES[t][half]
                        part = r3[:, 128 * half:128 * half + 128]
                        if (ox, oy) == (0, 0) and layer == c:
                            part = jnp.where(diag, 0.0, part)
                        else:
                            row_ref[col * 4 + layer] = row_ref[col * 4 + layer] + part
                        acc[c] = acc[c] + part.reshape(16, 8, 128).sum(0)
            for z in range(4):
                col_ref[(x * NY + y) * 4 + z] = acc[z]
        return carry

    lax.fori_loop(0, NY, dens, 0)
    def slope(y, carry):
        for x in range(NX):
            for z in range(4):
                v = row_ref[(x * (NY + 2) + y + 1) * 4 + z]
                other = jnp.sum(v.T.reshape(16, 8, 128), axis=0) + col_ref[(x * NY + y) * 4 + z]
                d = jnp.sum(other, axis=0, keepdims=True) * (1.0 / CUT ** 3)
                sl_ref[x, y, pl.ds(z, 1), :] = -0.5 / jnp.sqrt(d + 1.0)
        return carry

    lax.fori_loop(0, NY, slope, 0)

    def gprep(y, carry):
        for x in range(NX):
            for z in range(4):
                qx, qy, qz, _ = cell_rows(pos_ref, x, y, z + 1)
                s = jnp.broadcast_to(sl_ref[x, y, pl.ds(z, 1), :], (8, 128))
                v = pick(row % 4, qx, qy, qz, jnp.ones_like(qx))
                hi, mid, lo = split3(v * jnp.where(row < 4, 1.0, s))
                g_ref[(x * NY + y) * 4 + z] = jnp.concatenate([hi, mid, lo, jnp.zeros_like(hi)], 0).astype(BF)
        return carry

    lax.fori_loop(0, NY, gprep, 0)

    def force(n, carry):
        x = n // (8 // GROUP) + 1
        first = n % (8 // GROUP) * GROUP + 1
        zero = jnp.zeros((8, 128), F32)
        acc = [[[zero] * 4, [zero] * 4] for c in range(GROUP)]
        for ox in (-1, 0, 1):
            for oy in (-1, 0, 1):
                for c in range(GROUP):
                    y = first + c
                    col = (x + ox) * NY + y + oy
                    base = ((x + ox) * (NY + 2) + y + 1 + oy) * 3
                    for t, ca, cb in FORCE_TILES:
                        w = []
                        for half, z in ((0, ca), (1, cb)):
                            o = SHIFTS.index((ox, oy, TABLES[t][half] - z))
                            w.append(weights(cen_ref[(x * NY + y) * 4 + z], m_ref[o], k_ref[o]))
                        r = pair_values(te_ref[base + t], *w)
                        for half, z in ((0, ca), (1, cb)):
                            layer = TABLES[t][half]
                            shift = (ox, oy, layer - z)
                            p = r[:, 128 * half:128 * half + 128]
                            if shift == (0, 0, 0):
                                p = jnp.where(diag, 0.0, p)
                            p = p * p
                            hi = p.astype(BF)
                            lo = (p - hi.astype(F32)).astype(BF)
                            g = g_ref[col * 4 + layer]
                            f = dot(jnp.concatenate([g, g], 1), jnp.concatenate([hi, lo], 0))
                            f = f[0:8] + f[8:16] + f[16:24]
                            total = acc[c][z - 1]
                            total[0] = total[0] + f
                            for a in range(3):
                                if shift[a] == 1:
                                    total[a + 1] = total[a + 1] + f
                                elif shift[a] == -1:
                                    total[a + 1] = total[a + 1] - f
        for c, h in [(c, h) for c in range(GROUP) for h in range(2)]:
            y = first + c
            total = acc[c][h]
            rows = cell_rows(pos_ref, x, y, h + 2)
            s = sl_ref[x, y, pl.ds(h + 1, 1), :]
            sub = sub_ref[x - 1, y - 1, pl.ds(h, 1), :]
            both = diff_ref[pl.ds((y + 1) * 6 + 2 + h, 1), :]
            here = jnp.where(x == 1, both[:, 16:24], both[:, 24:32])
            heat = jnp.zeros((1, 128), F32)
            for kk in range(8):
                heat = jnp.where(sub == kk, here[:, kk:kk + 1], heat)
            for a in range(3):
                q = rows[a][0:1]
                plain = total[0][a:a + 1] + EDGE * total[1 + a][3:4] - q * total[0][3:4]
                sloped = total[0][4 + a:5 + a] + EDGE * total[1 + a][7:8] - q * total[0][7:8]
                f = (2.0 / CUT ** 2) * ((-3.0 / CUT) * (s * plain + sloped) + (-1.5 / CUT) * plain)
                v = vel_ref[a, x - 1, y - 1, pl.ds(h, 1), :]
                moved = v + 0.2 * f + 0.02 * heat * v
                out_ref[a, x - 1, y - 1, pl.ds(h, 1), :] = jnp.where(sub < 8, moved, 0.0)
        return carry

    lax.fori_loop(0, 16 // GROUP, force, 0)


def main_call(own, xb, xa, yb, ya, vel, sub, diff):
    m, k = shift_tables()
    return pl.pallas_call(
        main_kernel,
        out_shape=jax.ShapeDtypeStruct(vel.shape, F32),
        in_specs=[VM] * 10,
        out_specs=VM,
        scratch_shapes=[
            pltpu.VMEM((12, 10, 6, 128), F32),
            pltpu.VMEM((4 * 12 * 3, 128, 128), BF),
            pltpu.VMEM((160, 8, 128), F32),
            pltpu.VMEM((4, 10, 4, 128), F32),
            pltpu.VMEM((160, 32, 128), BF),
            pltpu.VMEM((4 * 12 * 4, 128, 128), F32),
            pltpu.VMEM((160, 8, 128), F32),
        ],
        compiler_params=pltpu.CompilerParams(vmem_limit_bytes=40 * 2 ** 20),
        name="pair_forces",
    )(own, xb, xa, yb, ya, vel, sub, diff, m, k)


def pack_kernel(own_ref, e_ref, xb_ref, xa_ref, up_ref, down_ref, mid_ref):
    lane = lax.broadcasted_iota(jnp.int32, (6, 128), 1)
    for y in range(8):
        lat = own_ref[6, y]
        mine = e_ref[y]
        e_part = jnp.where(lane < 16, pltpu.roll(xb_ref[3, y], 112, 1),
                           jnp.where(lane < 32, mine, pltpu.roll(xa_ref[3, y], 16, 1)))
        l_part = jnp.where(lane < 80, pltpu.roll(xb_ref[3, y], 64, 1),
                           jnp.where(lane < 96, pltpu.roll(lat, 80, 1), pltpu.roll(xa_ref[3, y], 96, 1)))
        used = (lane < 48) | ((lane >= 64) & (lane < 112))
        mid_ref[y] = jnp.where(used, jnp.where(lane < 64, e_part, l_part), 0.0)
    for ref, y in ((up_ref, 7), (down_ref, 0)):
        for a in range(3):
            ref[4 * a] = xb_ref[a, y]
            ref[4 * a + 1] = own_ref[2 * a, y]
            ref[4 * a + 2] = own_ref[2 * a + 1, y]
            ref[4 * a + 3] = xa_ref[a, y]
        for n in range(2):
            ref[12 + n] = mid_ref[(y // 7) * 6 + n]


def pack_call(own, e, xb, xa):
    message = jax.ShapeDtypeStruct((14, 6, 128), F32)
    return pl.pallas_call(
        pack_kernel,
        out_shape=(message, message, jax.ShapeDtypeStruct((8, 6, 128), F32)),
        in_specs=[VM] * 4,
        out_specs=(VM, VM, VM),
        compiler_params=pltpu.CompilerParams(vmem_limit_bytes=2 * 2 ** 20),
        name="pack",
    )(own, e, xb, xa)


def diffuse_kernel(mid_ref, yb_ref, ya_ref, e_out, diff_out, x_ref, e_ref):
    for n in range(2):
        x_ref[pl.ds(6 * n, 6)] = yb_ref[12 + n]
        x_ref[pl.ds(60 + 6 * n, 6)] = ya_ref[12 + n]
    for y in range(8):
        x_ref[pl.ds(12 + 6 * y, 6)] = mid_ref[y]
    rows = 72
    own = x_ref[...]
    lane = lax.broadcasted_iota(jnp.int32, (rows, 128), 1)
    lat = pltpu.roll(own, 64, 1)
    e = own
    e_ref[...] = jnp.zeros(e_ref.shape, F32)
    for step in range(4):
        e_ref[pl.ds(8, rows), :] = e
        beside = pltpu.roll(e, 4, 1) + pltpu.roll(e, 124, 1)
        for bit, stride in ((1, 1), (2, 6)):
            after = e_ref[pl.ds(8 + stride, rows), :]
            before = e_ref[pl.ds(8 - stride, rows), :]
            low = pltpu.roll(e + before, 128 - bit, 1)
            high = pltpu.roll(e + after, bit, 1)
            beside = beside + jnp.where((lane & bit) == 0, low, high)
        e = e + 0.15 * (beside - 6.0 * e) - 0.05 * (e - lat)
    e_ref[pl.ds(8, rows), :] = e
    for y in range(8):
        e_out[y] = e_ref[pl.ds(8 + 6 * (y + 2) + 2, 2), :]
    diff_out[...] = e - lat


def diffuse_call(mid, yb, ya):
    return pl.pallas_call(
        diffuse_kernel,
        out_shape=(jax.ShapeDtypeStruct((8, 2, 128), F32), jax.ShapeDtypeStruct((72, 128), F32)),
        in_specs=[VM] * 3,
        out_specs=(VM, VM),
        scratch_shapes=[pltpu.VMEM((72, 128), F32), pltpu.VMEM((88, 128), F32)],
        compiler_params=pltpu.CompilerParams(vmem_limit_bytes=2 * 2 ** 20),
        name="diffusion",
    )(mid, yb, ya)


def ring(value, axis, step):
    n = lax.axis_size(axis)
    return lax.ppermute(value, axis, [(i, (i + step) % n) for i in range(n)])


def per_device(positions, velocities, counts, grid_cells, electron_temp):
    nx, ny, nz = counts.shape
    slot = lax.broadcasted_iota(jnp.int32, grid_cells.shape, 3)
    occupied = slot < counts[..., None]
    shifted = [jnp.roll(electron_temp, 4, 2), electron_temp, jnp.roll(electron_temp, -4, 2)]
    e = lax.all_to_all(jnp.concatenate(shifted, 0), "gz", split_axis=2, concat_axis=1, tiled=True)
    e = e.reshape(3, 4, ny, 2, nz, 2).transpose(2, 0, 4, 1, 3, 5).reshape(ny, 6, 16)
    e = jnp.pad(e, ((0, 0), (0, 0), (16, 96)))
    kinetic = jnp.where(occupied, 0.5 * jnp.sum(velocities * velocities, axis=0), 0.0)
    sub = lax.broadcasted_iota(jnp.int32, (nx, ny, nz, 8, 128), 3)
    lat = jnp.sum(jnp.where(grid_cells[..., None, :] == sub, kinetic[..., None, :], 0.0), axis=-1)
    lat = lat.transpose(1, 2, 0, 3).reshape(1, ny, nz, 16)
    lat = jnp.pad(lat, ((0, 0), (0, 0), (0, 0), (0, 112)))
    parked = jnp.where(occupied[None], positions, 1000.0).reshape(6, ny, nz, 128)
    planes = jnp.concatenate([parked, lat], 0)
    own = jnp.concatenate([ring(planes, "gz", 1), planes, ring(planes, "gz", -1)], 2)
    field = (own[6] + e)[None]
    xb = ring(jnp.concatenate([own[1:6:2], field], 0), "gx", 1)
    xa = ring(jnp.concatenate([own[0:6:2], field], 0), "gx", -1)
    up, down, mid = pack_call(own, e, xb, xa)
    yb = ring(up, "gy", 1)
    ya = ring(down, "gy", -1)
    e_new, diff = diffuse_call(mid, yb, ya)
    heat = e_new[..., 16:32].reshape(ny, nz, 4, 2, 2).transpose(2, 0, 3, 1, 4).reshape(4, 2 * ny, 2 * nz)
    heat = lax.all_to_all(heat, "gz", split_axis=1, concat_axis=2, tiled=True)
    vel_out = main_call(own, xb, xa, yb, ya, velocities, jnp.where(occupied, grid_cells, 8), diff)
    return vel_out, heat


def solution(mesh):
    return jax.shard_map(
        per_device,
        mesh=mesh,
        in_specs=(
            P(None, "gx", "gy", "gz", None),
            P(None, "gx", "gy", "gz", None),
            P("gx", "gy", "gz"),
            P("gx", "gy", "gz", None),
            P("gx", ("gy", "gz"), None),
        ),
        out_specs=(P(None, "gx", "gy", "gz", None), P("gx", ("gy", "gz"), None)),
        check_vma=False,
    )
```

```python
import functools
import numpy as np
import jax
import jax.numpy as jnp
from jax import lax
from jax.experimental import pallas as pl
from jax.experimental.pallas import tpu as pltpu
from jax.sharding import PartitionSpec as P

CUT = 30.25
EDGE = 11.0
HALF = 5.5
BIG = 10000.0
GROUP = 4
F32 = jnp.float32
BF = jnp.bfloat16
VM = pl.BlockSpec(memory_space=pltpu.VMEM)
SHIFTS = [(x, y, z) for x in (-1, 0, 1) for y in (-1, 0, 1) for z in (-1, 0, 1)]


def split3(v):
    hi = v.astype(BF).astype(F32)
    rest = v - hi
    mid = rest.astype(BF).astype(F32)
    return hi, mid, rest - mid


def shift_tables():
    m = np.zeros((27, 8, 128), np.float32)
    k = np.zeros((27, 8, 128), np.float32)
    for n, o in enumerate(SHIFTS):
        m[n, 0:5] = 1.0
        for a in range(3):
            m[n, 5 + a] = o[a]
            k[n, a] = -2.0 * EDGE * o[a]
            k[n, 4] -= EDGE * EDGE * abs(o[a])
    return jnp.asarray(m), jnp.asarray(k)


def cell_rows(pos_ref, x, y, z):
    px = pos_ref[x, y, pl.ds(z, 1), :]
    py = pos_ref[4 + x, y, pl.ds(z, 1), :]
    pz = pos_ref[8 + x, y, pl.ds(z, 1), :]
    empty = px > 500.0
    qx = jnp.where(empty, 0.0, px - HALF)
    qy = jnp.where(empty, 0.0, py - HALF)
    qz = jnp.where(empty, 0.0, pz - HALF)
    s = jnp.where(empty, BIG, qx * qx + qy * qy + qz * qz)
    return [jnp.broadcast_to(v, (8, 128)) for v in (qx, qy, qz, s)]


def pick(row, *vals):
    out = vals[-1]
    for n in range(len(vals) - 2, -1, -1):
        out = jnp.where(row == n, vals[n], out)
    return out


def neighbour_block(row, rows):
    qx, qy, qz, s = rows
    hi, mid, lo = split3(pick(row, qx, qy, qz, s, jnp.float32(1.0), jnp.float32(2.0 * EDGE)))
    return jnp.concatenate([hi, mid, lo, hi, mid, hi, jnp.zeros_like(hi), jnp.zeros_like(hi)], axis=0)


def centre_block(row, rows):
    qx, qy, qz, s = rows
    return pick(row, 2.0 * qx, 2.0 * qy, 2.0 * qz, jnp.float32(-1.0), CUT - s, qx, qy, qz)


def weights(d, m, k):
    u1, u2, u3 = split3(d * m + k)
    z = jnp.zeros((16, 128), BF)
    c = lambda p, q: jnp.concatenate([p, q], axis=0).astype(BF)
    return jnp.concatenate([c(u1, u1), c(u1, u2), c(u2, u3), z], axis=0)


def dot(a, b):
    return jnp.dot(a, b, preferred_element_type=F32)


def pair_values(table, c0, c1):
    z = jnp.zeros((64, 128), BF)
    rhs = jnp.concatenate([jnp.concatenate([c0, z], 0), jnp.concatenate([z, c1], 0)], 1)
    return jnp.maximum(dot(table, rhs), 0.0)


def same_slot():
    return lax.broadcasted_iota(jnp.int32, (128, 128), 0) == lax.broadcasted_iota(jnp.int32, (128, 128), 1)


TABLES = ((0, 1), (2, 1), (2, 3))
DENSITY_TILES = ((0, 0, 1), (0, 1, 0), (1, 1, 2), (2, 2, 3), (2, 3, 2))
OWN_TILES = ((0, 0, 1), (2, 2, 3), (1, 1, 0), (2, None, 2))
FORCE_TILES = ((0, 1, 1), (1, 1, 2), (2, 2, 2))


def main_kernel(own_ref, xb_ref, xa_ref, yb_ref, ya_ref, vel_ref, sub_ref, diff_ref, m_ref, k_ref,
                out_ref, pos_ref, te_ref, cen_ref, sl_ref, g_ref, row_ref, col_ref):
    NX, NY = 4, 10
    row = lax.broadcasted_iota(jnp.int32, (8, 128), 0)
    low = lax.broadcasted_iota(jnp.int32, (128, 128), 1) < 64
    diag = same_slot()
    for a in range(3):
        for y in range(8):
            rows = pl.ds((a * 8 + y) * 4, 4)
            pos_ref[4 * a, y + 1] = xb_ref[rows]
            pos_ref[4 * a + 1, y + 1] = own_ref[2 * a, y, 1:5]
            pos_ref[4 * a + 2, y + 1] = own_ref[2 * a + 1, y, 1:5]
            pos_ref[4 * a + 3, y + 1] = xa_ref[rows]
    for p in range(12):
        pos_ref[p, 0] = yb_ref[pl.ds(4 * p, 4)]
        pos_ref[p, 9] = ya_ref[pl.ds(4 * p, 4)]

    def prep(y, carry):
        for x in range(NX):
            blocks = []
            for z in range(4):
                rows = cell_rows(pos_ref, x, y, z)
                blocks.append(neighbour_block(row, rows))
                cen_ref[(x * NY + y) * 4 + z] = centre_block(row, rows)
            a = jnp.concatenate(blocks[:2], 0).T
            b = jnp.concatenate(blocks[2:], 0).T
            base = (x * (NY + 2) + y + 1) * 3
            te_ref[base] = a.astype(BF)
            te_ref[base + 1] = jnp.where(low, b, a).astype(BF)
            te_ref[base + 2] = b.astype(BF)
        return carry

    lax.fori_loop(0, NY, prep, 0)
    for x in range(NX):
        for y in (0, NY + 1):
            te_ref[pl.ds((x * (NY + 2) + y) * 3, 3)] = jnp.zeros((3, 128, 128), BF)

    row_ref[...] = jnp.zeros(row_ref.shape, F32)

    def dens(y, carry):
        for x in range(NX):
            centres = [cen_ref[(x * NY + y) * 4 + z] for z in range(4)]
            acc = [jnp.zeros((8, 128), F32) for z in range(4)]
            for ox, oy in ((0, 0), (0, 1), (1, -1), (1, 0), (1, 1)):
                if x + ox >= NX:
                    continue
                col = (x + ox) * (NY + 2) + y + 1 + oy
                tiles = OWN_TILES if (ox, oy) == (0, 0) else DENSITY_TILES
                for t, ca, cb in tiles:
                    w = []
                    for half, c in ((0, ca), (1, cb)):
                        if c is None:
                            w.append(jnp.zeros((64, 128), BF))
                            continue
                        o = SHIFTS.index((ox, oy, TABLES[t][half] - c))
                        w.append(weights(centres[c], m_ref[o], k_ref[o]))
                    r = pair_values(te_ref[col * 3 + t], *w)
                    r3 = r * r * r
                    for half, c in ((0, ca), (1, cb)):
                        if c is None:
                            continue
                        layer = TABLES[t][half]
                        part = r3[:, 128 * half:128 * half + 128]
                        if (ox, oy) == (0, 0) and layer == c:
                            part = jnp.where(diag, 0.0, part)
                        else:
                            row_ref[col * 4 + layer] = row_ref[col * 4 + layer] + part
                        acc[c] = acc[c] + part.reshape(16, 8, 128).sum(0)
            for z in range(4):
                col_ref[(x * NY + y) * 4 + z] = acc[z]
        return carry

    lax.fori_loop(0, NY, dens, 0)
    def slope(y, carry):
        for x in range(NX):
            for z in range(4):
                v = row_ref[(x * (NY + 2) + y + 1) * 4 + z]
                other = jnp.sum(v.T.reshape(16, 8, 128), axis=0) + col_ref[(x * NY + y) * 4 + z]
                d = jnp.sum(other, axis=0, keepdims=True) * (1.0 / CUT ** 3)
                sl_ref[x, y, pl.ds(z, 1), :] = -0.5 / jnp.sqrt(d + 1.0)
        return carry

    lax.fori_loop(0, NY, slope, 0)

    def gprep(y, carry):
        for x in range(NX):
            for z in range(4):
                qx, qy, qz, _ = cell_rows(pos_ref, x, y, z)
                s = jnp.broadcast_to(sl_ref[x, y, pl.ds(z, 1), :], (8, 128))
                v = pick(row % 4, qx, qy, qz, jnp.ones_like(qx))
                hi, mid, lo = split3(v * jnp.where(row < 4, 1.0, s))
                g_ref[(x * NY + y) * 4 + z] = jnp.concatenate([hi, mid, lo, jnp.zeros_like(hi)], 0).astype(BF)
        return carry

    lax.fori_loop(0, NY, gprep, 0)

    def force(n, carry):
        x = n // (8 // GROUP) + 1
        first = n % (8 // GROUP) * GROUP + 1
        zero = jnp.zeros((8, 128), F32)
        acc = [[[zero] * 4, [zero] * 4] for c in range(GROUP)]
        for ox in (-1, 0, 1):
            for oy in (-1, 0, 1):
                for c in range(GROUP):
                    y = first + c
                    col = (x + ox) * NY + y + oy
                    base = ((x + ox) * (NY + 2) + y + 1 + oy) * 3
                    for t, ca, cb in FORCE_TILES:
                        w = []
                        for half, z in ((0, ca), (1, cb)):
                            o = SHIFTS.index((ox, oy, TABLES[t][half] - z))
                            w.append(weights(cen_ref[(x * NY + y) * 4 + z], m_ref[o], k_ref[o]))
                        r = pair_values(te_ref[base + t], *w)
                        for half, z in ((0, ca), (1, cb)):
                            layer = TABLES[t][half]
                            shift = (ox, oy, layer - z)
                            p = r[:, 128 * half:128 * half + 128]
                            if shift == (0, 0, 0):
                                p = jnp.where(diag, 0.0, p)
                            p = p * p
                            hi = p.astype(BF)
                            lo = (p - hi.astype(F32)).astype(BF)
                            g = g_ref[col * 4 + layer]
                            f = dot(jnp.concatenate([g, g], 1), jnp.concatenate([hi, lo], 0))
                            f = f[0:8] + f[8:16] + f[16:24]
                            total = acc[c][z - 1]
                            total[0] = total[0] + f
                            for a in range(3):
                                if shift[a] == 1:
                                    total[a + 1] = total[a + 1] + f
                                elif shift[a] == -1:
                                    total[a + 1] = total[a + 1] - f
        for c, h in [(c, h) for c in range(GROUP) for h in range(2)]:
            y = first + c
            total = acc[c][h]
            rows = cell_rows(pos_ref, x, y, h + 1)
            s = sl_ref[x, y, pl.ds(h + 1, 1), :]
            sub = sub_ref[x - 1, y - 1, pl.ds(h, 1), :]
            both = diff_ref[pl.ds((y + 1) * 6 + 2 + h, 1), :]
            here = jnp.where(x == 1, both[:, 16:24], both[:, 24:32])
            heat = jnp.zeros((1, 128), F32)
            for kk in range(8):
                heat = jnp.where(sub == kk, here[:, kk:kk + 1], heat)
            for a in range(3):
                q = rows[a][0:1]
                plain = total[0][a:a + 1] + EDGE * total[1 + a][3:4] - q * total[0][3:4]
                sloped = total[0][4 + a:5 + a] + EDGE * total[1 + a][7:8] - q * total[0][7:8]
                f = (2.0 / CUT ** 2) * ((-3.0 / CUT) * (s * plain + sloped) + (-1.5 / CUT) * plain)
                v = vel_ref[a, x - 1, y - 1, pl.ds(h, 1), :]
                moved = v + 0.2 * f + 0.02 * heat * v
                out_ref[a, x - 1, y - 1, pl.ds(h, 1), :] = jnp.where(sub < 8, moved, 0.0)
        return carry

    lax.fori_loop(0, 16 // GROUP, force, 0)


def main_call(own, xb, xa, yb, ya, vel, sub, diff):
    m, k = shift_tables()
    return pl.pallas_call(
        main_kernel,
        out_shape=jax.ShapeDtypeStruct(vel.shape, F32),
        in_specs=[VM] * 10,
        out_specs=VM,
        scratch_shapes=[
            pltpu.VMEM((12, 10, 4, 128), F32),
            pltpu.VMEM((4 * 12 * 3, 128, 128), BF),
            pltpu.VMEM((160, 8, 128), F32),
            pltpu.VMEM((4, 10, 4, 128), F32),
            pltpu.VMEM((160, 32, 128), BF),
            pltpu.VMEM((4 * 12 * 4, 128, 128), F32),
            pltpu.VMEM((160, 8, 128), F32),
        ],
        compiler_params=pltpu.CompilerParams(vmem_limit_bytes=40 * 2 ** 20),
        name="pair_forces",
    )(own, xb, xa, yb, ya, vel, sub, diff, m, k)


SMALL = pltpu.CompilerParams(vmem_limit_bytes=2 * 2 ** 20)


def rows_of(n):
    return jax.ShapeDtypeStruct((n, 128), F32)


def front_kernel(cnt_ref, pos_ref, vel_ref, grid_ref, own_ref, up_ref, down_ref):
    lane = lax.broadcasted_iota(jnp.int32, (2, 128), 1)
    first = lax.broadcasted_iota(jnp.int32, (2, 128), 0) == 0
    for y in range(8):
        lat = jnp.zeros((2, 128), F32)
        for x in range(2):
            occupied = lane < jnp.where(first, cnt_ref[x, y, 0], cnt_ref[x, y, 1])
            for a in range(3):
                p = jnp.where(occupied, pos_ref[a, x, y], 1000.0)
                plane = 2 * a + x
                own_ref[plane, y] = p
                down_ref[pl.ds(plane * 8 + y, 1)] = p[0:1]
                up_ref[pl.ds(plane * 8 + y, 1)] = p[1:2]
            v = [vel_ref[a, x, y] for a in range(3)]
            kinetic = jnp.where(occupied, 0.5 * (v[0] * v[0] + v[1] * v[1] + v[2] * v[2]), 0.0)
            sub = grid_ref[x, y]
            for k in range(8):
                total = jnp.sum(jnp.where(sub == k, kinetic, 0.0), axis=1, keepdims=True)
                lat = jnp.where(lane == 8 * x + k, total, lat)
        own_ref[6, y] = lat
        down_ref[pl.ds(48 + 2 * y, 2)] = lat
        up_ref[pl.ds(48 + 2 * y, 2)] = lat


def front_call(counts, positions, velocities, grid_cells):
    return pl.pallas_call(
        front_kernel,
        out_shape=(jax.ShapeDtypeStruct((7, 8, 2, 128), F32), rows_of(64), rows_of(64)),
        in_specs=[pl.BlockSpec(memory_space=pltpu.SMEM)] + [VM] * 3,
        out_specs=(VM, VM, VM),
        compiler_params=SMALL,
        name="front",
    )(counts, positions, velocities, grid_cells)


def pack_x_kernel(mine_ref, zb_ref, za_ref, e_ref, own_ref, up_ref, down_ref):
    for y in range(8):
        for plane in range(6):
            row = pl.ds(plane * 8 + y, 1)
            own_ref[plane, y, 1:2] = zb_ref[row]
            own_ref[plane, y, 2:4] = mine_ref[plane, y]
            own_ref[plane, y, 4:5] = za_ref[row]
            message = down_ref if plane % 2 == 0 else up_ref
            base = (plane // 2 * 8 + y) * 4
            message[pl.ds(base, 1)] = zb_ref[row]
            message[pl.ds(base + 1, 2)] = mine_ref[plane, y]
            message[pl.ds(base + 3, 1)] = za_ref[row]
        pair = pl.ds(48 + 2 * y, 2)
        own_ref[6, y, 0:2] = zb_ref[pair]
        own_ref[6, y, 2:4] = mine_ref[6, y]
        own_ref[6, y, 4:6] = za_ref[pair]
        field = own_ref[6, y] + e_ref[y]
        up_ref[pl.ds(96 + 6 * y, 6)] = field
        down_ref[pl.ds(96 + 6 * y, 6)] = field


def pack_x_call(mine, zb, za, e):
    return pl.pallas_call(
        pack_x_kernel,
        out_shape=(jax.ShapeDtypeStruct((7, 8, 6, 128), F32), rows_of(144), rows_of(144)),
        in_specs=[VM] * 4,
        out_specs=(VM, VM, VM),
        compiler_params=SMALL,
        name="pack_x",
    )(mine, zb, za, e)


def pack_y_kernel(own_ref, e_ref, xb_ref, xa_ref, up_ref, down_ref, mid_ref):
    lane = lax.broadcasted_iota(jnp.int32, (6, 128), 1)
    used = (lane < 48) | ((lane >= 64) & (lane < 112))
    for y in range(8):
        before, after = xb_ref[pl.ds(96 + 6 * y, 6)], xa_ref[pl.ds(96 + 6 * y, 6)]
        lat, e = own_ref[6, y], e_ref[y]
        e_part = jnp.where(lane < 16, pltpu.roll(before, 112, 1), jnp.where(lane < 32, e, pltpu.roll(after, 16, 1)))
        l_part = jnp.where(lane < 80, pltpu.roll(before, 64, 1),
                           jnp.where(lane < 96, pltpu.roll(lat, 80, 1), pltpu.roll(after, 96, 1)))
        mid_ref[y] = jnp.where(used, jnp.where(lane < 64, e_part, l_part), 0.0)
    for ref, y in ((up_ref, 7), (down_ref, 0)):
        for a in range(3):
            rows = pl.ds((a * 8 + y) * 4, 4)
            ref[pl.ds(16 * a, 4)] = xb_ref[rows]
            ref[pl.ds(16 * a + 4, 4)] = own_ref[2 * a, y, 1:5]
            ref[pl.ds(16 * a + 8, 4)] = own_ref[2 * a + 1, y, 1:5]
            ref[pl.ds(16 * a + 12, 4)] = xa_ref[rows]
        for n in range(2):
            ref[pl.ds(48 + 6 * n, 6)] = mid_ref[(y // 7) * 6 + n]
        ref[pl.ds(60, 4)] = jnp.zeros((4, 128), F32)


def pack_y_call(own, e, xb, xa):
    return pl.pallas_call(
        pack_y_kernel,
        out_shape=(rows_of(64), rows_of(64), jax.ShapeDtypeStruct((8, 6, 128), F32)),
        in_specs=[VM] * 4,
        out_specs=(VM, VM, VM),
        compiler_params=SMALL,
        name="pack_y",
    )(own, e, xb, xa)


def diffuse_kernel(mid_ref, yb_ref, ya_ref, e_out, diff_out, x_ref, e_ref):
    for n in range(2):
        x_ref[pl.ds(6 * n, 6)] = yb_ref[pl.ds(48 + 6 * n, 6)]
        x_ref[pl.ds(60 + 6 * n, 6)] = ya_ref[pl.ds(48 + 6 * n, 6)]
    for y in range(8):
        x_ref[pl.ds(12 + 6 * y, 6)] = mid_ref[y]
    rows = 72
    own = x_ref[...]
    lane = lax.broadcasted_iota(jnp.int32, (rows, 128), 1)
    lat = pltpu.roll(own, 64, 1)
    e = own
    e_ref[...] = jnp.zeros(e_ref.shape, F32)
    for step in range(4):
        e_ref[pl.ds(8, rows), :] = e
        beside = pltpu.roll(e, 4, 1) + pltpu.roll(e, 124, 1)
        for bit, stride in ((1, 1), (2, 6)):
            after = e_ref[pl.ds(8 + stride, rows), :]
            before = e_ref[pl.ds(8 - stride, rows), :]
            low = pltpu.roll(e + before, 128 - bit, 1)
            high = pltpu.roll(e + after, bit, 1)
            beside = beside + jnp.where((lane & bit) == 0, low, high)
        e = e + 0.15 * (beside - 6.0 * e) - 0.05 * (e - lat)
    e_ref[pl.ds(8, rows), :] = e
    for y in range(8):
        e_out[y] = e_ref[pl.ds(8 + 6 * (y + 2) + 2, 2), :]
    diff_out[...] = e - lat


def diffuse_call(mid, yb, ya):
    return pl.pallas_call(
        diffuse_kernel,
        out_shape=(jax.ShapeDtypeStruct((8, 2, 128), F32), jax.ShapeDtypeStruct((72, 128), F32)),
        in_specs=[VM] * 3,
        out_specs=(VM, VM),
        scratch_shapes=[pltpu.VMEM((72, 128), F32), pltpu.VMEM((88, 128), F32)],
        compiler_params=SMALL,
        name="diffusion",
    )(mid, yb, ya)


def ring(value, axis, step):
    n = lax.axis_size(axis)
    return lax.ppermute(value, axis, [(i, (i + step) % n) for i in range(n)])


def per_device(positions, velocities, counts, grid_cells, electron_temp):
    nx, ny, nz = counts.shape
    slot = lax.broadcasted_iota(jnp.int32, grid_cells.shape, 3)
    occupied = slot < counts[..., None]
    shifted = [jnp.roll(electron_temp, 4, 2), electron_temp, jnp.roll(electron_temp, -4, 2)]
    e = lax.all_to_all(jnp.concatenate(shifted, 0), "gz", split_axis=2, concat_axis=1, tiled=True)
    e = e.reshape(3, 4, ny, 2, nz, 2).transpose(2, 0, 4, 1, 3, 5).reshape(ny, 6, 16)
    e = jnp.pad(e, ((0, 0), (0, 0), (16, 96)))
    mine, up, down = front_call(counts, positions, velocities, grid_cells)
    own, up, down = pack_x_call(mine, ring(up, "gz", 1), ring(down, "gz", -1), e)
    xb, xa = ring(up, "gx", 1), ring(down, "gx", -1)
    up, down, mid = pack_y_call(own, e, xb, xa)
    yb, ya = ring(up, "gy", 1), ring(down, "gy", -1)
    e_new, diff = diffuse_call(mid, yb, ya)
    heat = e_new[..., 16:32].reshape(ny, nz, 4, 2, 2).transpose(2, 0, 3, 1, 4).reshape(4, 2 * ny, 2 * nz)
    heat = lax.all_to_all(heat, "gz", split_axis=1, concat_axis=2, tiled=True)
    vel_out = main_call(own, xb, xa, yb, ya, velocities, jnp.where(occupied, grid_cells, 8), diff)
    return vel_out, heat


def solution(mesh):
    return jax.shard_map(
        per_device,
        mesh=mesh,
        in_specs=(
            P(None, "gx", "gy", "gz", None),
            P(None, "gx", "gy", "gz", None),
            P("gx", "gy", "gz"),
            P("gx", "gy", "gz", None),
            P("gx", ("gy", "gz"), None),
        ),
        out_specs=(P(None, "gx", "gy", "gz", None), P("gx", ("gy", "gz"), None)),
        check_vma=False,
    )
```

```python
import functools
import numpy as np
import jax
import jax.numpy as jnp
from jax import lax
from jax.experimental import pallas as pl
from jax.experimental.pallas import tpu as pltpu
from jax.sharding import PartitionSpec as P

CUT = 30.25
EDGE = 11.0
HALF = 5.5
BIG = 10000.0
GROUP = 8
F32 = jnp.float32
BF = jnp.bfloat16
VM = pl.BlockSpec(memory_space=pltpu.VMEM)
SHIFTS = [(x, y, z) for x in (-1, 0, 1) for y in (-1, 0, 1) for z in (-1, 0, 1)]


def split3(v):
    hi = v.astype(BF).astype(F32)
    rest = v - hi
    mid = rest.astype(BF).astype(F32)
    return hi, mid, rest - mid


def shift_tables():
    m = np.zeros((27, 8, 128), np.float32)
    k = np.zeros((27, 8, 128), np.float32)
    for n, o in enumerate(SHIFTS):
        m[n, 0:5] = 1.0
        for a in range(3):
            m[n, 5 + a] = o[a]
            k[n, a] = -2.0 * EDGE * o[a]
            k[n, 4] -= EDGE * EDGE * abs(o[a])
    return jnp.asarray(m), jnp.asarray(k)


def cell_rows(pos_ref, x, y, z):
    px = pos_ref[x, y, pl.ds(z, 1), :]
    py = pos_ref[4 + x, y, pl.ds(z, 1), :]
    pz = pos_ref[8 + x, y, pl.ds(z, 1), :]
    empty = px > 500.0
    qx = jnp.where(empty, 0.0, px - HALF)
    qy = jnp.where(empty, 0.0, py - HALF)
    qz = jnp.where(empty, 0.0, pz - HALF)
    s = jnp.where(empty, BIG, qx * qx + qy * qy + qz * qz)
    return [jnp.broadcast_to(v, (8, 128)) for v in (qx, qy, qz, s)]


def pick(row, *vals):
    out = vals[-1]
    for n in range(len(vals) - 2, -1, -1):
        out = jnp.where(row == n, vals[n], out)
    return out


def neighbour_block(row, rows):
    qx, qy, qz, s = rows
    hi, mid, lo = split3(pick(row, qx, qy, qz, s, jnp.float32(1.0), jnp.float32(2.0 * EDGE)))
    return jnp.concatenate([hi, mid, lo, hi, mid, hi, jnp.zeros_like(hi), jnp.zeros_like(hi)], axis=0)


def centre_block(row, rows):
    qx, qy, qz, s = rows
    return pick(row, 2.0 * qx, 2.0 * qy, 2.0 * qz, jnp.float32(-1.0), CUT - s, qx, qy, qz)


def weights(d, m, k):
    u1, u2, u3 = split3(d * m + k)
    z = jnp.zeros((16, 128), BF)
    c = lambda p, q: jnp.concatenate([p, q], axis=0).astype(BF)
    return jnp.concatenate([c(u1, u1), c(u1, u2), c(u2, u3), z], axis=0)


def dot(a, b):
    return jnp.dot(a, b, preferred_element_type=F32)


def pair_values(table, c0, c1):
    z = jnp.zeros((64, 128), BF)
    rhs = jnp.concatenate([jnp.concatenate([c0, z], 0), jnp.concatenate([z, c1], 0)], 1)
    return jnp.maximum(dot(table, rhs), 0.0)


def same_slot():
    return lax.broadcasted_iota(jnp.int32, (128, 128), 0) == lax.broadcasted_iota(jnp.int32, (128, 128), 1)


TABLES = ((0, 1), (2, 1), (2, 3))
DENSITY_TILES = ((0, 0, 1), (0, 1, 0), (1, 1, 2), (2, 2, 3), (2, 3, 2))
OWN_TILES = ((0, 0, 1), (2, 2, 3), (1, 1, 0), (2, None, 2))
FORCE_TILES = ((0, 1, 1), (1, 1, 2), (2, 2, 2))


def main_kernel(own_ref, xb_ref, xa_ref, yb_ref, ya_ref, vel_ref, sub_ref, diff_ref, m_ref, k_ref,
                out_ref, pos_ref, te_ref, cen_ref, sl_ref, g_ref, row_ref, col_ref):
    NX, NY = 4, 10
    row = lax.broadcasted_iota(jnp.int32, (8, 128), 0)
    low = lax.broadcasted_iota(jnp.int32, (128, 128), 1) < 64
    diag = same_slot()
    for a in range(3):
        for y in range(8):
            rows = pl.ds((a * 8 + y) * 4, 4)
            pos_ref[4 * a, y + 1] = xb_ref[rows]
            pos_ref[4 * a + 1, y + 1] = own_ref[2 * a, y, 1:5]
            pos_ref[4 * a + 2, y + 1] = own_ref[2 * a + 1, y, 1:5]
            pos_ref[4 * a + 3, y + 1] = xa_ref[rows]
    for p in range(12):
        pos_ref[p, 0] = yb_ref[pl.ds(4 * p, 4)]
        pos_ref[p, 9] = ya_ref[pl.ds(4 * p, 4)]

    def prep(y, carry):
        for x in range(NX):
            blocks = []
            for z in range(4):
                rows = cell_rows(pos_ref, x, y, z)
                blocks.append(neighbour_block(row, rows))
                cen_ref[(x * NY + y) * 4 + z] = centre_block(row, rows)
            a = jnp.concatenate(blocks[:2], 0).T
            b = jnp.concatenate(blocks[2:], 0).T
            base = (x * (NY + 2) + y + 1) * 3
            te_ref[base] = a.astype(BF)
            te_ref[base + 1] = jnp.where(low, b, a).astype(BF)
            te_ref[base + 2] = b.astype(BF)
        return carry

    lax.fori_loop(0, NY, prep, 0)
    for x in range(NX):
        for y in (0, NY + 1):
            te_ref[pl.ds((x * (NY + 2) + y) * 3, 3)] = jnp.zeros((3, 128, 128), BF)

    row_ref[...] = jnp.zeros(row_ref.shape, F32)

    def dens(y, carry):
        for x in range(NX):
            centres = [cen_ref[(x * NY + y) * 4 + z] for z in range(4)]
            acc = [jnp.zeros((8, 128), F32) for z in range(4)]
            for ox, oy in ((0, 0), (0, 1), (1, -1), (1, 0), (1, 1)):
                if x + ox >= NX:
                    continue
                col = (x + ox) * (NY + 2) + y + 1 + oy
                tiles = OWN_TILES if (ox, oy) == (0, 0) else DENSITY_TILES
                for t, ca, cb in tiles:
                    w = []
                    for half, c in ((0, ca), (1, cb)):
                        if c is None:
                            w.append(jnp.zeros((64, 128), BF))
                            continue
                        o = SHIFTS.index((ox, oy, TABLES[t][half] - c))
                        w.append(weights(centres[c], m_ref[o], k_ref[o]))
                    r = pair_values(te_ref[col * 3 + t], *w)
                    r3 = r * r * r
                    for half, c in ((0, ca), (1, cb)):
                        if c is None:
                            continue
                        layer = TABLES[t][half]
                        part = r3[:, 128 * half:128 * half + 128]
                        if (ox, oy) == (0, 0) and layer == c:
                            part = jnp.where(diag, 0.0, part)
                        else:
                            row_ref[col * 4 + layer] = row_ref[col * 4 + layer] + part
                        acc[c] = acc[c] + part.reshape(16, 8, 128).sum(0)
            for z in range(4):
                col_ref[(x * NY + y) * 4 + z] = acc[z]
        return carry

    lax.fori_loop(0, NY, dens, 0)
    def slope(y, carry):
        for x in range(NX):
            for z in range(4):
                v = row_ref[(x * (NY + 2) + y + 1) * 4 + z]
                other = jnp.sum(v.T.reshape(16, 8, 128), axis=0) + col_ref[(x * NY + y) * 4 + z]
                d = jnp.sum(other, axis=0, keepdims=True) * (1.0 / CUT ** 3)
                sl_ref[x, y, pl.ds(z, 1), :] = -0.5 / jnp.sqrt(d + 1.0)
        return carry

    lax.fori_loop(0, NY, slope, 0)

    def gprep(y, carry):
        for x in range(NX):
            for z in range(4):
                qx, qy, qz, _ = cell_rows(pos_ref, x, y, z)
                s = jnp.broadcast_to(sl_ref[x, y, pl.ds(z, 1), :], (8, 128))
                v = pick(row % 4, qx, qy, qz, jnp.ones_like(qx))
                hi, mid, lo = split3(v * jnp.where(row < 4, 1.0, s))
                g_ref[(x * NY + y) * 4 + z] = jnp.concatenate([hi, mid, lo, jnp.zeros_like(hi)], 0).astype(BF)
        return carry

    lax.fori_loop(0, NY, gprep, 0)

    def force(n, carry):
        x = n // (8 // GROUP) + 1
        first = n % (8 // GROUP) * GROUP + 1
        zero = jnp.zeros((8, 128), F32)
        acc = [[[zero] * 4, [zero] * 4] for c in range(GROUP)]
        for ox in (-1, 0, 1):
            for oy in (-1, 0, 1):
                for c in range(GROUP):
                    y = first + c
                    col = (x + ox) * NY + y + oy
                    base = ((x + ox) * (NY + 2) + y + 1 + oy) * 3
                    for t, ca, cb in FORCE_TILES:
                        w = []
                        for half, z in ((0, ca), (1, cb)):
                            o = SHIFTS.index((ox, oy, TABLES[t][half] - z))
                            w.append(weights(cen_ref[(x * NY + y) * 4 + z], m_ref[o], k_ref[o]))
                        r = pair_values(te_ref[base + t], *w)
                        for half, z in ((0, ca), (1, cb)):
                            layer = TABLES[t][half]
                            shift = (ox, oy, layer - z)
                            p = r[:, 128 * half:128 * half + 128]
                            if shift == (0, 0, 0):
                                p = jnp.where(diag, 0.0, p)
                            p = p * p
                            hi = p.astype(BF)
                            lo = (p - hi.astype(F32)).astype(BF)
                            g = g_ref[col * 4 + layer]
                            f = dot(jnp.concatenate([g, g], 1), jnp.concatenate([hi, lo], 0))
                            f = f[0:8] + f[8:16] + f[16:24]
                            total = acc[c][z - 1]
                            total[0] = total[0] + f
                            for a in range(3):
                                if shift[a] == 1:
                                    total[a + 1] = total[a + 1] + f
                                elif shift[a] == -1:
                                    total[a + 1] = total[a + 1] - f
        for c, h in [(c, h) for c in range(GROUP) for h in range(2)]:
            y = first + c
            total = acc[c][h]
            rows = cell_rows(pos_ref, x, y, h + 1)
            s = sl_ref[x, y, pl.ds(h + 1, 1), :]
            sub = sub_ref[x - 1, y - 1, pl.ds(h, 1), :]
            both = diff_ref[pl.ds((y + 1) * 6 + 2 + h, 1), :]
            here = jnp.where(x == 1, both[:, 16:24], both[:, 24:32])
            heat = jnp.zeros((1, 128), F32)
            for kk in range(8):
                heat = jnp.where(sub == kk, here[:, kk:kk + 1], heat)
            for a in range(3):
                q = rows[a][0:1]
                plain = total[0][a:a + 1] + EDGE * total[1 + a][3:4] - q * total[0][3:4]
                sloped = total[0][4 + a:5 + a] + EDGE * total[1 + a][7:8] - q * total[0][7:8]
                f = (2.0 / CUT ** 2) * ((-3.0 / CUT) * (s * plain + sloped) + (-1.5 / CUT) * plain)
                v = vel_ref[a, x - 1, y - 1, pl.ds(h, 1), :]
                moved = v + 0.2 * f + 0.02 * heat * v
                out_ref[a, x - 1, y - 1, pl.ds(h, 1), :] = jnp.where(sub < 8, moved, 0.0)
        return carry

    lax.fori_loop(0, 16 // GROUP, force, 0)


def main_call(own, xb, xa, yb, ya, vel, sub, diff):
    m, k = shift_tables()
    return pl.pallas_call(
        main_kernel,
        out_shape=jax.ShapeDtypeStruct(vel.shape, F32),
        in_specs=[VM] * 10,
        out_specs=VM,
        scratch_shapes=[
            pltpu.VMEM((12, 10, 4, 128), F32),
            pltpu.VMEM((4 * 12 * 3, 128, 128), BF),
            pltpu.VMEM((160, 8, 128), F32),
            pltpu.VMEM((4, 10, 4, 128), F32),
            pltpu.VMEM((160, 32, 128), BF),
            pltpu.VMEM((4 * 12 * 4, 128, 128), F32),
            pltpu.VMEM((160, 8, 128), F32),
        ],
        compiler_params=pltpu.CompilerParams(vmem_limit_bytes=40 * 2 ** 20),
        name="pair_forces",
    )(own, xb, xa, yb, ya, vel, sub, diff, m, k)


SMALL = pltpu.CompilerParams(vmem_limit_bytes=2 * 2 ** 20)


def rows_of(n):
    return jax.ShapeDtypeStruct((n, 128), F32)


def front_kernel(cnt_ref, pos_ref, vel_ref, grid_ref, own_ref, up_ref, down_ref):
    lane = lax.broadcasted_iota(jnp.int32, (2, 128), 1)
    first = lax.broadcasted_iota(jnp.int32, (2, 128), 0) == 0
    for y in range(8):
        lat = jnp.zeros((2, 128), F32)
        for x in range(2):
            occupied = lane < jnp.where(first, cnt_ref[x, y, 0], cnt_ref[x, y, 1])
            for a in range(3):
                p = jnp.where(occupied, pos_ref[a, x, y], 1000.0)
                plane = 2 * a + x
                own_ref[plane, y] = p
                down_ref[pl.ds(plane * 8 + y, 1)] = p[0:1]
                up_ref[pl.ds(plane * 8 + y, 1)] = p[1:2]
            v = [vel_ref[a, x, y] for a in range(3)]
            kinetic = jnp.where(occupied, 0.5 * (v[0] * v[0] + v[1] * v[1] + v[2] * v[2]), 0.0)
            sub = grid_ref[x, y]
            for k in range(8):
                total = jnp.sum(jnp.where(sub == k, kinetic, 0.0), axis=1, keepdims=True)
                lat = jnp.where(lane == 8 * x + k, total, lat)
        own_ref[6, y] = lat
        down_ref[pl.ds(48 + 2 * y, 2)] = lat
        up_ref[pl.ds(48 + 2 * y, 2)] = lat


def front_call(counts, positions, velocities, grid_cells):
    return pl.pallas_call(
        front_kernel,
        out_shape=(jax.ShapeDtypeStruct((7, 8, 2, 128), F32), rows_of(64), rows_of(64)),
        in_specs=[pl.BlockSpec(memory_space=pltpu.SMEM)] + [VM] * 3,
        out_specs=(VM, VM, VM),
        compiler_params=SMALL,
        name="front",
    )(counts, positions, velocities, grid_cells)


def pack_x_kernel(mine_ref, zb_ref, za_ref, e_ref, own_ref, up_ref, down_ref):
    for y in range(8):
        for plane in range(6):
            row = pl.ds(plane * 8 + y, 1)
            own_ref[plane, y, 1:2] = zb_ref[row]
            own_ref[plane, y, 2:4] = mine_ref[plane, y]
            own_ref[plane, y, 4:5] = za_ref[row]
            message = down_ref if plane % 2 == 0 else up_ref
            base = (plane // 2 * 8 + y) * 4
            message[pl.ds(base, 1)] = zb_ref[row]
            message[pl.ds(base + 1, 2)] = mine_ref[plane, y]
            message[pl.ds(base + 3, 1)] = za_ref[row]
        pair = pl.ds(48 + 2 * y, 2)
        own_ref[6, y, 0:2] = zb_ref[pair]
        own_ref[6, y, 2:4] = mine_ref[6, y]
        own_ref[6, y, 4:6] = za_ref[pair]
        field = own_ref[6, y] + e_ref[y]
        up_ref[pl.ds(96 + 6 * y, 6)] = field
        down_ref[pl.ds(96 + 6 * y, 6)] = field


def pack_x_call(mine, zb, za, e):
    return pl.pallas_call(
        pack_x_kernel,
        out_shape=(jax.ShapeDtypeStruct((7, 8, 6, 128), F32), rows_of(144), rows_of(144)),
        in_specs=[VM] * 4,
        out_specs=(VM, VM, VM),
        compiler_params=SMALL,
        name="pack_x",
    )(mine, zb, za, e)


def pack_y_kernel(own_ref, e_ref, xb_ref, xa_ref, up_ref, down_ref, mid_ref):
    lane = lax.broadcasted_iota(jnp.int32, (6, 128), 1)
    used = (lane < 48) | ((lane >= 64) & (lane < 112))
    for y in range(8):
        before, after = xb_ref[pl.ds(96 + 6 * y, 6)], xa_ref[pl.ds(96 + 6 * y, 6)]
        lat, e = own_ref[6, y], e_ref[y]
        e_part = jnp.where(lane < 16, pltpu.roll(before, 112, 1), jnp.where(lane < 32, e, pltpu.roll(after, 16, 1)))
        l_part = jnp.where(lane < 80, pltpu.roll(before, 64, 1),
                           jnp.where(lane < 96, pltpu.roll(lat, 80, 1), pltpu.roll(after, 96, 1)))
        mid_ref[y] = jnp.where(used, jnp.where(lane < 64, e_part, l_part), 0.0)
    for ref, y in ((up_ref, 7), (down_ref, 0)):
        for a in range(3):
            rows = pl.ds((a * 8 + y) * 4, 4)
            ref[pl.ds(16 * a, 4)] = xb_ref[rows]
            ref[pl.ds(16 * a + 4, 4)] = own_ref[2 * a, y, 1:5]
            ref[pl.ds(16 * a + 8, 4)] = own_ref[2 * a + 1, y, 1:5]
            ref[pl.ds(16 * a + 12, 4)] = xa_ref[rows]
        for n in range(2):
            ref[pl.ds(48 + 6 * n, 6)] = mid_ref[(y // 7) * 6 + n]
        ref[pl.ds(60, 4)] = jnp.zeros((4, 128), F32)


def pack_y_call(own, e, xb, xa):
    return pl.pallas_call(
        pack_y_kernel,
        out_shape=(rows_of(64), rows_of(64), jax.ShapeDtypeStruct((8, 6, 128), F32)),
        in_specs=[VM] * 4,
        out_specs=(VM, VM, VM),
        compiler_params=SMALL,
        name="pack_y",
    )(own, e, xb, xa)


def diffuse_kernel(mid_ref, yb_ref, ya_ref, e_out, diff_out, x_ref, e_ref):
    for n in range(2):
        x_ref[pl.ds(6 * n, 6)] = yb_ref[pl.ds(48 + 6 * n, 6)]
        x_ref[pl.ds(60 + 6 * n, 6)] = ya_ref[pl.ds(48 + 6 * n, 6)]
    for y in range(8):
        x_ref[pl.ds(12 + 6 * y, 6)] = mid_ref[y]
    rows = 72
    own = x_ref[...]
    lane = lax.broadcasted_iota(jnp.int32, (rows, 128), 1)
    lat = pltpu.roll(own, 64, 1)
    e = own
    e_ref[...] = jnp.zeros(e_ref.shape, F32)
    for step in range(4):
        e_ref[pl.ds(8, rows), :] = e
        beside = pltpu.roll(e, 4, 1) + pltpu.roll(e, 124, 1)
        for bit, stride in ((1, 1), (2, 6)):
            after = e_ref[pl.ds(8 + stride, rows), :]
            before = e_ref[pl.ds(8 - stride, rows), :]
            low = pltpu.roll(e + before, 128 - bit, 1)
            high = pltpu.roll(e + after, bit, 1)
            beside = beside + jnp.where((lane & bit) == 0, low, high)
        e = e + 0.15 * (beside - 6.0 * e) - 0.05 * (e - lat)
    e_ref[pl.ds(8, rows), :] = e
    for y in range(8):
        e_out[y] = e_ref[pl.ds(8 + 6 * (y + 2) + 2, 2), :]
    diff_out[...] = e - lat


def diffuse_call(mid, yb, ya):
    return pl.pallas_call(
        diffuse_kernel,
        out_shape=(jax.ShapeDtypeStruct((8, 2, 128), F32), jax.ShapeDtypeStruct((72, 128), F32)),
        in_specs=[VM] * 3,
        out_specs=(VM, VM),
        scratch_shapes=[pltpu.VMEM((72, 128), F32), pltpu.VMEM((88, 128), F32)],
        compiler_params=SMALL,
        name="diffusion",
    )(mid, yb, ya)


def ring(value, axis, step):
    n = lax.axis_size(axis)
    return lax.ppermute(value, axis, [(i, (i + step) % n) for i in range(n)])


def per_device(positions, velocities, counts, grid_cells, electron_temp):
    nx, ny, nz = counts.shape
    slot = lax.broadcasted_iota(jnp.int32, grid_cells.shape, 3)
    occupied = slot < counts[..., None]
    shifted = [jnp.roll(electron_temp, 4, 2), electron_temp, jnp.roll(electron_temp, -4, 2)]
    e = lax.all_to_all(jnp.concatenate(shifted, 0), "gz", split_axis=2, concat_axis=1, tiled=True)
    mine, up, down = front_call(counts, positions, velocities, grid_cells)
    up, down, e = lax.optimization_barrier((up, down, e))
    e = e.reshape(3, 4, ny, 2, nz, 2).transpose(2, 0, 4, 1, 3, 5).reshape(ny, 6, 16)
    e = jnp.pad(e, ((0, 0), (0, 0), (16, 96)))
    own, up, down = pack_x_call(mine, ring(up, "gz", 1), ring(down, "gz", -1), e)
    xb, xa = ring(up, "gx", 1), ring(down, "gx", -1)
    up, down, mid = pack_y_call(own, e, xb, xa)
    yb, ya = ring(up, "gy", 1), ring(down, "gy", -1)
    e_new, diff = diffuse_call(mid, yb, ya)
    heat = e_new[..., 16:32].reshape(ny, nz, 4, 2, 2).transpose(2, 0, 3, 1, 4).reshape(4, 2 * ny, 2 * nz)
    heat = lax.all_to_all(heat, "gz", split_axis=1, concat_axis=2, tiled=True)
    vel_out = main_call(own, xb, xa, yb, ya, velocities, jnp.where(occupied, grid_cells, 8), diff)
    return vel_out, heat


def solution(mesh):
    return jax.shard_map(
        per_device,
        mesh=mesh,
        in_specs=(
            P(None, "gx", "gy", "gz", None),
            P(None, "gx", "gy", "gz", None),
            P("gx", "gy", "gz"),
            P("gx", "gy", "gz", None),
            P("gx", ("gy", "gz"), None),
        ),
        out_specs=(P(None, "gx", "gy", "gz", None), P("gx", ("gy", "gz"), None)),
        check_vma=False,
    )
```

```python
import functools
import numpy as np
import jax
import jax.numpy as jnp
from jax import lax
from jax.experimental import pallas as pl
from jax.experimental.pallas import tpu as pltpu
from jax.sharding import PartitionSpec as P

CUT = 30.25
EDGE = 11.0
HALF = 5.5
BIG = 10000.0
GROUP = 8
F32 = jnp.float32
BF = jnp.bfloat16
VM = pl.BlockSpec(memory_space=pltpu.VMEM)
SHIFTS = [(x, y, z) for x in (-1, 0, 1) for y in (-1, 0, 1) for z in (-1, 0, 1)]


def split3(v):
    hi = v.astype(BF).astype(F32)
    rest = v - hi
    mid = rest.astype(BF).astype(F32)
    return hi, mid, rest - mid


def shift_tables():
    m = np.zeros((27, 8, 128), np.float32)
    k = np.zeros((27, 8, 128), np.float32)
    for n, o in enumerate(SHIFTS):
        m[n, 0:5] = 1.0
        for a in range(3):
            m[n, 5 + a] = o[a]
            k[n, a] = -2.0 * EDGE * o[a]
            k[n, 4] -= EDGE * EDGE * abs(o[a])
    return jnp.asarray(m), jnp.asarray(k)


def cell_rows(pos_ref, x, y, z):
    px = pos_ref[x, y, pl.ds(z, 1), :]
    py = pos_ref[4 + x, y, pl.ds(z, 1), :]
    pz = pos_ref[8 + x, y, pl.ds(z, 1), :]
    empty = px > 500.0
    qx = jnp.where(empty, 0.0, px - HALF)
    qy = jnp.where(empty, 0.0, py - HALF)
    qz = jnp.where(empty, 0.0, pz - HALF)
    s = jnp.where(empty, BIG, qx * qx + qy * qy + qz * qz)
    return [jnp.broadcast_to(v, (8, 128)) for v in (qx, qy, qz, s)]


def pick(row, *vals):
    out = vals[-1]
    for n in range(len(vals) - 2, -1, -1):
        out = jnp.where(row == n, vals[n], out)
    return out


def neighbour_block(row, rows):
    qx, qy, qz, s = rows
    hi, mid, lo = split3(pick(row, qx, qy, qz, s, jnp.float32(1.0), jnp.float32(2.0 * EDGE)))
    return jnp.concatenate([hi, mid, lo, hi, mid, hi, jnp.zeros_like(hi), jnp.zeros_like(hi)], axis=0)


def centre_block(row, rows):
    qx, qy, qz, s = rows
    return pick(row, 2.0 * qx, 2.0 * qy, 2.0 * qz, jnp.float32(-1.0), CUT - s, qx, qy, qz)


def weights(d, m, k):
    u1, u2, u3 = split3(d * m + k)
    z = jnp.zeros((16, 128), BF)
    c = lambda p, q: jnp.concatenate([p, q], axis=0).astype(BF)
    return jnp.concatenate([c(u1, u1), c(u1, u2), c(u2, u3), z], axis=0)


def dot(a, b):
    return jnp.dot(a, b, preferred_element_type=F32)


def pair_values(table, c0, c1):
    z = jnp.zeros((64, 128), BF)
    rhs = jnp.concatenate([jnp.concatenate([c0, z], 0), jnp.concatenate([z, c1], 0)], 1)
    return jnp.maximum(dot(table, rhs), 0.0)


def same_slot():
    return lax.broadcasted_iota(jnp.int32, (128, 128), 0) == lax.broadcasted_iota(jnp.int32, (128, 128), 1)


TABLES = ((0, 1), (2, 1), (2, 3))
DENSITY_TILES = ((0, 0, 1), (0, 1, 0), (1, 1, 2), (2, 2, 3), (2, 3, 2))
OWN_TILES = ((0, 0, 1), (2, 2, 3), (1, 1, 0), (2, None, 2))
FORCE_TILES = ((0, 1, 1), (1, 1, 2), (2, 2, 2))


def main_kernel(own_ref, xb_ref, xa_ref, yb_ref, ya_ref, vel_ref, sub_ref, diff_ref, m_ref, k_ref,
                out_ref, pos_ref, te_ref, cen_ref, sl_ref, g_ref, row_ref, col_ref):
    NX, NY = 4, 10
    row = lax.broadcasted_iota(jnp.int32, (8, 128), 0)
    low = lax.broadcasted_iota(jnp.int32, (128, 128), 1) < 64
    diag = same_slot()
    for a in range(3):
        for y in range(8):
            rows = pl.ds((a * 8 + y) * 4, 4)
            pos_ref[4 * a, y + 1] = xb_ref[rows]
            pos_ref[4 * a + 1, y + 1] = own_ref[2 * a, y, 1:5]
            pos_ref[4 * a + 2, y + 1] = own_ref[2 * a + 1, y, 1:5]
            pos_ref[4 * a + 3, y + 1] = xa_ref[rows]
    for p in range(12):
        pos_ref[p, 0] = yb_ref[pl.ds(4 * p, 4)]
        pos_ref[p, 9] = ya_ref[pl.ds(4 * p, 4)]

    def prep(y, carry):
        for x in range(NX):
            blocks = []
            for z in range(4):
                rows = cell_rows(pos_ref, x, y, z)
                blocks.append(neighbour_block(row, rows))
                cen_ref[(x * NY + y) * 4 + z] = centre_block(row, rows)
            a = jnp.concatenate(blocks[:2], 0).T
            b = jnp.concatenate(blocks[2:], 0).T
            base = (x * (NY + 2) + y + 1) * 3
            te_ref[base] = a.astype(BF)
            te_ref[base + 1] = jnp.where(low, b, a).astype(BF)
            te_ref[base + 2] = b.astype(BF)
        return carry

    lax.fori_loop(0, NY, prep, 0)
    for x in range(NX):
        for y in (0, NY + 1):
            te_ref[pl.ds((x * (NY + 2) + y) * 3, 3)] = jnp.zeros((3, 128, 128), BF)

    row_ref[...] = jnp.zeros(row_ref.shape, F32)

    def dens(y, carry):
        for x in range(NX):
            centres = [cen_ref[(x * NY + y) * 4 + z] for z in range(4)]
            acc = [jnp.zeros((8, 128), F32) for z in range(4)]
            for ox, oy in ((0, 0), (0, 1), (1, -1), (1, 0), (1, 1)):
                if x + ox >= NX:
                    continue
                col = (x + ox) * (NY + 2) + y + 1 + oy
                tiles = OWN_TILES if (ox, oy) == (0, 0) else DENSITY_TILES
                for t, ca, cb in tiles:
                    w = []
                    for half, c in ((0, ca), (1, cb)):
                        if c is None:
                            w.append(jnp.zeros((64, 128), BF))
                            continue
                        o = SHIFTS.index((ox, oy, TABLES[t][half] - c))
                        w.append(weights(centres[c], m_ref[o], k_ref[o]))
                    r = pair_values(te_ref[col * 3 + t], *w)
                    r3 = r * r * r
                    for half, c in ((0, ca), (1, cb)):
                        if c is None:
                            continue
                        layer = TABLES[t][half]
                        part = r3[:, 128 * half:128 * half + 128]
                        if (ox, oy) == (0, 0) and layer == c:
                            part = jnp.where(diag, 0.0, part)
                        else:
                            row_ref[col * 4 + layer] = row_ref[col * 4 + layer] + part
                        acc[c] = acc[c] + part.reshape(16, 8, 128).sum(0)
            for z in range(4):
                col_ref[(x * NY + y) * 4 + z] = acc[z]
        return carry

    lax.fori_loop(0, NY, dens, 0)
    def slope(y, carry):
        for x in range(NX):
            for z in range(4):
                v = row_ref[(x * (NY + 2) + y + 1) * 4 + z]
                other = jnp.sum(v.T.reshape(16, 8, 128), axis=0) + col_ref[(x * NY + y) * 4 + z]
                d = jnp.sum(other, axis=0, keepdims=True) * (1.0 / CUT ** 3)
                sl_ref[x, y, pl.ds(z, 1), :] = -0.5 / jnp.sqrt(d + 1.0)
        return carry

    lax.fori_loop(0, NY, slope, 0)

    def gprep(y, carry):
        for x in range(NX):
            for z in range(4):
                qx, qy, qz, _ = cell_rows(pos_ref, x, y, z)
                s = jnp.broadcast_to(sl_ref[x, y, pl.ds(z, 1), :], (8, 128))
                v = pick(row % 4, qx, qy, qz, jnp.ones_like(qx))
                hi, mid, lo = split3(v * jnp.where(row < 4, 1.0, s))
                g_ref[(x * NY + y) * 4 + z] = jnp.concatenate([hi, mid, lo, jnp.zeros_like(hi)], 0).astype(BF)
        return carry

    lax.fori_loop(0, NY, gprep, 0)

    def force(n, carry):
        x = n // (8 // GROUP) + 1
        first = n % (8 // GROUP) * GROUP + 1
        zero = jnp.zeros((8, 128), F32)
        acc = [[[zero] * 4, [zero] * 4] for c in range(GROUP)]
        for ox in (-1, 0, 1):
            for oy in (-1, 0, 1):
                for c in range(GROUP):
                    y = first + c
                    col = (x + ox) * NY + y + oy
                    base = ((x + ox) * (NY + 2) + y + 1 + oy) * 3
                    for t, ca, cb in FORCE_TILES:
                        w = []
                        for half, z in ((0, ca), (1, cb)):
                            o = SHIFTS.index((ox, oy, TABLES[t][half] - z))
                            w.append(weights(cen_ref[(x * NY + y) * 4 + z], m_ref[o], k_ref[o]))
                        r = pair_values(te_ref[base + t], *w)
                        for half, z in ((0, ca), (1, cb)):
                            layer = TABLES[t][half]
                            shift = (ox, oy, layer - z)
                            p = r[:, 128 * half:128 * half + 128]
                            if shift == (0, 0, 0):
                                p = jnp.where(diag, 0.0, p)
                            p = p * p
                            hi = p.astype(BF)
                            lo = (p - hi.astype(F32)).astype(BF)
                            g = g_ref[col * 4 + layer]
                            f = dot(jnp.concatenate([g, g], 1), jnp.concatenate([hi, lo], 0))
                            f = f[0:8] + f[8:16] + f[16:24]
                            total = acc[c][z - 1]
                            total[0] = total[0] + f
                            for a in range(3):
                                if shift[a] == 1:
                                    total[a + 1] = total[a + 1] + f
                                elif shift[a] == -1:
                                    total[a + 1] = total[a + 1] - f
        for c, h in [(c, h) for c in range(GROUP) for h in range(2)]:
            y = first + c
            total = acc[c][h]
            rows = cell_rows(pos_ref, x, y, h + 1)
            s = sl_ref[x, y, pl.ds(h + 1, 1), :]
            sub = sub_ref[x - 1, y - 1, pl.ds(h, 1), :]
            both = diff_ref[pl.ds((y + 1) * 6 + 2 + h, 1), :]
            here = jnp.where(x == 1, both[:, 16:24], both[:, 24:32])
            heat = jnp.zeros((1, 128), F32)
            for kk in range(8):
                heat = jnp.where(sub == kk, here[:, kk:kk + 1], heat)
            for a in range(3):
                q = rows[a][0:1]
                plain = total[0][a:a + 1] + EDGE * total[1 + a][3:4] - q * total[0][3:4]
                sloped = total[0][4 + a:5 + a] + EDGE * total[1 + a][7:8] - q * total[0][7:8]
                f = (2.0 / CUT ** 2) * ((-3.0 / CUT) * (s * plain + sloped) + (-1.5 / CUT) * plain)
                v = vel_ref[a, x - 1, y - 1, pl.ds(h, 1), :]
                moved = v + 0.2 * f + 0.02 * heat * v
                out_ref[a, x - 1, y - 1, pl.ds(h, 1), :] = jnp.where(sub < 8, moved, 0.0)
        return carry

    lax.fori_loop(0, 16 // GROUP, force, 0)


def main_call(own, xb, xa, yb, ya, vel, sub, diff):
    m, k = shift_tables()
    return pl.pallas_call(
        main_kernel,
        out_shape=jax.ShapeDtypeStruct(vel.shape, F32),
        in_specs=[VM] * 10,
        out_specs=VM,
        scratch_shapes=[
            pltpu.VMEM((12, 10, 4, 128), F32),
            pltpu.VMEM((4 * 12 * 3, 128, 128), BF),
            pltpu.VMEM((160, 8, 128), F32),
            pltpu.VMEM((4, 10, 4, 128), F32),
            pltpu.VMEM((160, 32, 128), BF),
            pltpu.VMEM((4 * 12 * 4, 128, 128), F32),
            pltpu.VMEM((160, 8, 128), F32),
        ],
        compiler_params=pltpu.CompilerParams(vmem_limit_bytes=40 * 2 ** 20),
        name="pair_forces",
    )(own, xb, xa, yb, ya, vel, sub, diff, m, k)


SMALL = pltpu.CompilerParams(vmem_limit_bytes=2 * 2 ** 20)


def rows_of(n):
    return jax.ShapeDtypeStruct((n, 128), F32)


def front_kernel(cnt_ref, pos_ref, vel_ref, grid_ref, own_ref, up_ref, down_ref):
    lane = lax.broadcasted_iota(jnp.int32, (2, 128), 1)
    first = lax.broadcasted_iota(jnp.int32, (2, 128), 0) == 0
    for y in range(8):
        lat = jnp.zeros((2, 128), F32)
        for x in range(2):
            occupied = lane < jnp.where(first, cnt_ref[x, y, 0], cnt_ref[x, y, 1])
            for a in range(3):
                p = jnp.where(occupied, pos_ref[a, x, y], 1000.0)
                plane = 2 * a + x
                own_ref[plane, y] = p
                down_ref[pl.ds(plane * 8 + y, 1)] = p[0:1]
                up_ref[pl.ds(plane * 8 + y, 1)] = p[1:2]
            v = [vel_ref[a, x, y] for a in range(3)]
            kinetic = jnp.where(occupied, 0.5 * (v[0] * v[0] + v[1] * v[1] + v[2] * v[2]), 0.0)
            sub = grid_ref[x, y]
            for k in range(8):
                total = jnp.sum(jnp.where(sub == k, kinetic, 0.0), axis=1, keepdims=True)
                lat = jnp.where(lane == 8 * x + k, total, lat)
        own_ref[6, y] = lat
        down_ref[pl.ds(48 + 2 * y, 2)] = lat
        up_ref[pl.ds(48 + 2 * y, 2)] = lat


def front_call(counts, positions, velocities, grid_cells):
    return pl.pallas_call(
        front_kernel,
        out_shape=(jax.ShapeDtypeStruct((7, 8, 2, 128), F32), rows_of(64), rows_of(64)),
        in_specs=[pl.BlockSpec(memory_space=pltpu.SMEM)] + [VM] * 3,
        out_specs=(VM, VM, VM),
        compiler_params=SMALL,
        name="front",
    )(counts, positions, velocities, grid_cells)


def pack_x_kernel(mine_ref, zb_ref, za_ref, e_ref, own_ref, up_ref, down_ref):
    for y in range(8):
        for plane in range(6):
            row = pl.ds(plane * 8 + y, 1)
            own_ref[plane, y, 1:2] = zb_ref[row]
            own_ref[plane, y, 2:4] = mine_ref[plane, y]
            own_ref[plane, y, 4:5] = za_ref[row]
            message = down_ref if plane % 2 == 0 else up_ref
            base = (plane // 2 * 8 + y) * 4
            message[pl.ds(base, 1)] = zb_ref[row]
            message[pl.ds(base + 1, 2)] = mine_ref[plane, y]
            message[pl.ds(base + 3, 1)] = za_ref[row]
        pair = pl.ds(48 + 2 * y, 2)
        own_ref[6, y, 0:2] = zb_ref[pair]
        own_ref[6, y, 2:4] = mine_ref[6, y]
        own_ref[6, y, 4:6] = za_ref[pair]
        field = own_ref[6, y] + e_ref[y]
        up_ref[pl.ds(96 + 6 * y, 6)] = field
        down_ref[pl.ds(96 + 6 * y, 6)] = field


def pack_x_call(mine, zb, za, e):
    return pl.pallas_call(
        pack_x_kernel,
        out_shape=(jax.ShapeDtypeStruct((7, 8, 6, 128), F32), rows_of(144), rows_of(144)),
        in_specs=[VM] * 4,
        out_specs=(VM, VM, VM),
        compiler_params=SMALL,
        name="pack_x",
    )(mine, zb, za, e)


def pack_y_kernel(own_ref, e_ref, xb_ref, xa_ref, up_ref, down_ref, mid_ref):
    lane = lax.broadcasted_iota(jnp.int32, (6, 128), 1)
    used = (lane < 48) | ((lane >= 64) & (lane < 112))
    for y in range(8):
        before, after = xb_ref[pl.ds(96 + 6 * y, 6)], xa_ref[pl.ds(96 + 6 * y, 6)]
        lat, e = own_ref[6, y], e_ref[y]
        e_part = jnp.where(lane < 16, pltpu.roll(before, 112, 1), jnp.where(lane < 32, e, pltpu.roll(after, 16, 1)))
        l_part = jnp.where(lane < 80, pltpu.roll(before, 64, 1),
                           jnp.where(lane < 96, pltpu.roll(lat, 80, 1), pltpu.roll(after, 96, 1)))
        mid_ref[y] = jnp.where(used, jnp.where(lane < 64, e_part, l_part), 0.0)
    for ref, y in ((up_ref, 7), (down_ref, 0)):
        for a in range(3):
            rows = pl.ds((a * 8 + y) * 4, 4)
            ref[pl.ds(16 * a, 4)] = xb_ref[rows]
            ref[pl.ds(16 * a + 4, 4)] = own_ref[2 * a, y, 1:5]
            ref[pl.ds(16 * a + 8, 4)] = own_ref[2 * a + 1, y, 1:5]
            ref[pl.ds(16 * a + 12, 4)] = xa_ref[rows]
        for n in range(2):
            ref[pl.ds(48 + 6 * n, 6)] = mid_ref[(y // 7) * 6 + n]
        ref[pl.ds(60, 4)] = jnp.zeros((4, 128), F32)


def pack_y_call(own, e, xb, xa):
    return pl.pallas_call(
        pack_y_kernel,
        out_shape=(rows_of(64), rows_of(64), jax.ShapeDtypeStruct((8, 6, 128), F32)),
        in_specs=[VM] * 4,
        out_specs=(VM, VM, VM),
        compiler_params=SMALL,
        name="pack_y",
    )(own, e, xb, xa)


def diffuse_kernel(mid_ref, yb_ref, ya_ref, e_out, diff_out, x_ref, e_ref):
    for n in range(2):
        x_ref[pl.ds(6 * n, 6)] = yb_ref[pl.ds(48 + 6 * n, 6)]
        x_ref[pl.ds(60 + 6 * n, 6)] = ya_ref[pl.ds(48 + 6 * n, 6)]
    for y in range(8):
        x_ref[pl.ds(12 + 6 * y, 6)] = mid_ref[y]
    rows = 72
    own = x_ref[...]
    lane = lax.broadcasted_iota(jnp.int32, (rows, 128), 1)
    lat = pltpu.roll(own, 64, 1)
    e = own
    e_ref[...] = jnp.zeros(e_ref.shape, F32)
    for step in range(4):
        e_ref[pl.ds(8, rows), :] = e
        beside = pltpu.roll(e, 4, 1) + pltpu.roll(e, 124, 1)
        for bit, stride in ((1, 1), (2, 6)):
            after = e_ref[pl.ds(8 + stride, rows), :]
            before = e_ref[pl.ds(8 - stride, rows), :]
            low = pltpu.roll(e + before, 128 - bit, 1)
            high = pltpu.roll(e + after, bit, 1)
            beside = beside + jnp.where((lane & bit) == 0, low, high)
        e = e + 0.15 * (beside - 6.0 * e) - 0.05 * (e - lat)
    e_ref[pl.ds(8, rows), :] = e
    for y in range(8):
        e_out[y] = e_ref[pl.ds(8 + 6 * (y + 2) + 2, 2), :]
    diff_out[...] = e - lat


def diffuse_call(mid, yb, ya):
    return pl.pallas_call(
        diffuse_kernel,
        out_shape=(jax.ShapeDtypeStruct((8, 2, 128), F32), jax.ShapeDtypeStruct((72, 128), F32)),
        in_specs=[VM] * 3,
        out_specs=(VM, VM),
        scratch_shapes=[pltpu.VMEM((72, 128), F32), pltpu.VMEM((88, 128), F32)],
        compiler_params=SMALL,
        name="diffusion",
    )(mid, yb, ya)


def ring(value, axis, step):
    n = lax.axis_size(axis)
    return lax.ppermute(value, axis, [(i, (i + step) % n) for i in range(n)])


def per_device(positions, velocities, counts, grid_cells, electron_temp):
    nx, ny, nz = counts.shape
    slot = lax.broadcasted_iota(jnp.int32, grid_cells.shape, 3)
    occupied = slot < counts[..., None]
    shifted = [jnp.roll(electron_temp, 4, 2), electron_temp, jnp.roll(electron_temp, -4, 2)]
    e = lax.all_to_all(jnp.concatenate(shifted, 0), "gz", split_axis=2, concat_axis=1, tiled=True)
    e = e.reshape(3, 4, ny, 2, nz, 2).transpose(2, 0, 4, 1, 3, 5).reshape(ny, 6, 16)
    e = jnp.pad(e, ((0, 0), (0, 0), (16, 96)))
    mine, up, down = front_call(counts, positions, velocities, grid_cells)
    own, up, down = pack_x_call(mine, ring(up, "gz", 1), ring(down, "gz", -1), e)
    xb, xa = ring(up, "gx", 1), ring(down, "gx", -1)
    up, down, mid = pack_y_call(own, e, xb, xa)
    yb, ya = ring(up, "gy", 1), ring(down, "gy", -1)
    e_new, diff = diffuse_call(mid, yb, ya)
    heat = e_new[..., 16:32].reshape(ny, nz, 4, 2, 2).transpose(2, 0, 3, 1, 4).reshape(4, 2 * ny, 2 * nz)
    heat = lax.all_to_all(heat, "gz", split_axis=1, concat_axis=2, tiled=True)
    vel_out = main_call(own, xb, xa, yb, ya, velocities, jnp.where(occupied, grid_cells, 8), diff)
    return vel_out, heat


def solution(mesh):
    return jax.shard_map(
        per_device,
        mesh=mesh,
        in_specs=(
            P(None, "gx", "gy", "gz", None),
            P(None, "gx", "gy", "gz", None),
            P("gx", "gy", "gz"),
            P("gx", "gy", "gz", None),
            P("gx", ("gy", "gz"), None),
        ),
        out_specs=(P(None, "gx", "gy", "gz", None), P("gx", ("gy", "gz"), None)),
        check_vma=False,
    )
```
